32 devices in a mesh: fsdp: 2 (over x), ctx: 4 (over y, core), tp: 4 (over z).
Axes of the slice: x: 2, y: 2, z: 4, core: 2. Of those that a mesh axis runs over, the one named last changes fastest.
Arguments:
- prompt_in: bfloat16 [4, 1024, 2048], P('fsdp', 'ctx', 'tp'), may hold values from -6 to 6
- cont_in: bfloat16 [16, 128, 2048], P(('fsdp', 'ctx'), None, 'tp'), may hold values from -6 to 6
- prompt_mask: int32 [4, 1024], P('fsdp', 'ctx'), may hold values 0 or 1
- cont_mask: int32 [16, 128], P(('fsdp', 'ctx')), may hold values 0 or 1
- cont_prompt: int32 [16], P(('fsdp', 'ctx')), may hold values from 0 to 3, as said below
- cont_start: int32 [16], P(('fsdp', 'ctx')), may hold values from 1024 to 2047
- gain_attn: bfloat16 [2048], P('tp'), may hold values from 0.5 to 1.5
- gain_ffn: bfloat16 [2048], P('tp'), may hold values from 0.5 to 1.5
- router: bfloat16 [2048], P('tp'), may hold values from -0.125 to 0.125
- w_query: bfloat16 [2048, 2048], P('fsdp', 'tp'), may hold values from -0.125 to 0.125
- key_projection: bfloat16 [2048, 512], P('fsdp', 'tp'), may hold values from -0.125 to 0.125
- w_value: bfloat16 [2048, 512], P('fsdp', 'tp'), may hold values from -0.125 to 0.125
- w_out: bfloat16 [2048, 2048], P('tp', 'fsdp'), may hold values from -1.5 to 1.5
- w_gate: bfloat16 [2048, 8192], P('fsdp', 'tp'), may hold values from -0.125 to 0.125
- w_up: bfloat16 [2048, 8192], P('fsdp', 'tp'), may hold values from -0.125 to 0.125
- w_down: bfloat16 [8192, 2048], P('tp', 'fsdp'), may hold values from -0.0625 to 0.0625
- prompt_cot: bfloat16 [4, 1024, 2048], P('fsdp', 'ctx', 'tp'), may hold values from -6 to 6
- cont_cot: bfloat16 [16, 128, 2048], P(('fsdp', 'ctx'), None, 'tp'), may hold values from -6 to 6
Outputs:
- prompt_out: bfloat16 [4, 1024, 2048], P('fsdp', 'ctx', 'tp')
- cont_out: bfloat16 [16, 128, 2048], P(('fsdp', 'ctx'), None, 'tp')
- prompt_grad: float32 [4, 1024, 2048], P('fsdp', 'ctx', 'tp')
- cont_grad: float32 [16, 128, 2048], P(('fsdp', 'ctx'), None, 'tp')
- grad_gain_attn: float32 [2048], P('tp')
- grad_gain_ffn: float32 [2048], P('tp')
- grad_router: float32 [2048], P('tp')
- grad_query: float32 [2048, 2048], P('fsdp', 'tp')
- grad_key: float32 [2048, 512], P('fsdp', 'tp')
- grad_value: float32 [2048, 512], P('fsdp', 'tp')
- grad_out: float32 [2048, 2048], P('tp', 'fsdp')
- grad_gate: float32 [2048, 8192], P('fsdp', 'tp')
- grad_up: float32 [2048, 8192], P('fsdp', 'tp')
- grad_down: float32 [8192, 2048], P('tp', 'fsdp')
The draws below stay inside these ranges and needn't reach their ends.
Inputs may be any that keep to these rules, and one draw needn't show every extreme that they name: `cont_prompt`: continuation c names a prompt of its own block: (c // 8) * 2 plus a value below 2; each prompt is named by exactly 4 continuations.
All inputs are finite; a program needn't handle non-finite values. No bound on the sum of `prompt_mask` or of `cont_mask` on one device may be relied on, other than what follows from the above.
Results may differ from the reference program's by a relative error of at most 0.014.
Values may be sent and summed in bfloat16 or wider, within the bound.
No kernel may reach another device: no remote copies, remote signals or barrier semaphores. Data moves between devices by JAX's collectives and lax.ppermute only.
A program may use at most 256 MiB of HBM per device.

```python
from functools import partial
import jax
import jax.numpy as jnp
from jax import lax

D = 2048
FF = 8192
QUERY_HEAD_COUNT = 32
KEY_VALUE_HEADS = 8
HEAD_SIZE = 64
PROMPT_LENGTH = 1024
CONTINUATION_LEN = 128
G_DEV = 2
QW = 2048
KW = 512
GROUPS = 4
CONT_BLOCK = 8
CONTS = 16
N_FSDP = 2


def draw_cont_prompt(key, part):
    block_count = CONTS // CONT_BLOCK
    block_keys = jax.random.split(key, block_count)
    orders = jax.vmap(lambda block_key: jax.random.permutation(block_key, CONT_BLOCK))(block_keys)
    chosen = orders.astype(jnp.int32) % G_DEV + jnp.arange(block_count, dtype=jnp.int32)[:, None] * G_DEV
    return chosen.reshape(CONTS).astype(jnp.int32)


def set_ends(drawn, key, smallest, largest):
    shape = drawn.shape
    index_at = [jax.random.randint(jax.random.fold_in(key, axis), (), 0, shape[axis]) for axis in range(len(shape))]
    drawn = drawn.at[tuple(index_at)].set(smallest)
    longest = shape.index(max(shape))
    index_at[longest] = (index_at[longest] + 1) % shape[longest]
    return drawn.at[tuple(index_at)].set(largest)


def block_levels(stream_key, dims, cuts, smallest, high):
    def one(dim, parts):
        heights = jax.random.uniform(jax.random.fold_in(jax.random.fold_in(stream_key, 6), dim), (parts,), jnp.float32, smallest / len(cuts), high / len(cuts))
        return jnp.repeat(jnp.exp(heights), dims[dim] // parts).reshape((-1,) + (1,) * (len(dims) - dim - 1))

    factor_of = one(*cuts[0])
    for cut in cuts[1:]:
        factor_of = factor_of * one(*cut)
    return factor_of


def centred(key, shape, width, limit, cuts=(), kind=jnp.bfloat16):
    array = jax.random.normal(key, shape, jnp.float32) * width
    if len(cuts) > 0:
        array = block_levels(key, shape, cuts, -0.22, 0.18) * array
    return jnp.clip(array, min=-limit, max=limit).astype(kind)


def setup_inputs(seed: int = 0) -> dict:
    streams_of = jax.random.split(jax.random.key(seed), 19)
    return {
        "prompt_in": centred(streams_of[0], (GROUPS, PROMPT_LENGTH, D), 1.0, 6.0, ((0, 2), (1, 4), (2, 4))),
        "cont_in": centred(streams_of[1], (CONTS, CONTINUATION_LEN, D), 1.0, 6.0, ((0, 8), (2, 4))),
        "prompt_mask": set_ends((jax.random.randint(streams_of[2], (GROUPS, PROMPT_LENGTH), 0, 3) < 2).astype(jnp.int32), jax.random.fold_in(streams_of[2], 1), 0, 1),
        "cont_mask": set_ends((jax.random.randint(streams_of[3], (CONTS, CONTINUATION_LEN), 0, 3) < 2).astype(jnp.int32), jax.random.fold_in(streams_of[3], 1), 0, 1),
        "cont_prompt": draw_cont_prompt(jax.random.fold_in(streams_of[18], 71), 0),
        "cont_start": set_ends(jax.random.randint(streams_of[5], (CONTS,), PROMPT_LENGTH, 2 * PROMPT_LENGTH), jax.random.fold_in(streams_of[5], 1), PROMPT_LENGTH, (2 * PROMPT_LENGTH) - 1).astype(jnp.int32),
        "gain_attn": jnp.clip(1.0 + 0.1 * jax.random.normal(streams_of[6], (D,), jnp.float32), 0.5, 1.5).astype(jnp.bfloat16),
        "gain_ffn": jnp.clip(1.0 + 0.1 * jax.random.normal(streams_of[7], (D,), jnp.float32), 0.5, 1.5).astype(jnp.bfloat16),
        "router": centred(streams_of[8], (D,), D ** -0.5, 0.125, ((0, 4),)),
        "w_query": centred(streams_of[9], (D, QW), D ** -0.5, 0.125, ((0, 2), (1, 4))),
        "key_projection": centred(streams_of[10], (D, KW), D ** -0.5, 0.125, ((0, 2), (1, 4))),
        "w_value": centred(streams_of[11], (D, KW), D ** -0.5, 0.125, ((0, 2), (1, 4))),
        "w_out": centred(streams_of[12], (QW, D), (max(QW // 128, 1)) ** -0.5, 1.5, ((0, 4), (1, 2))),
        "w_gate": centred(streams_of[13], (D, FF), D ** -0.5, 0.125, ((0, 2), (1, 4))),
        "w_up": centred(streams_of[14], (D, FF), D ** -0.5, 0.125, ((0, 2), (1, 4))),
        "w_down": centred(streams_of[15], (FF, D), FF ** -0.5, 0.0625, ((0, 4), (1, 2))),
        "prompt_cot": centred(streams_of[16], (GROUPS, PROMPT_LENGTH, D), 1.0, 6.0, ((0, 2), (1, 4), (2, 4))),
        "cont_cot": centred(streams_of[17], (CONTS, CONTINUATION_LEN, D), 1.0, 6.0, ((0, 8), (2, 4))),
    }


@jax.custom_vjp
def reduced_precision(v):
    return lax.optimization_barrier(v.astype(jnp.bfloat16)).astype(jnp.float32)

@jax.custom_vjp
def reduced_precision_backward(v):
    return v

def low_keep(v):
    return (reduced_precision(v), None)

def low_pass(kept, grad):
    return (grad,)

def back_keep(v):
    return (v, None)

def back_low(kept, grad):
    return (reduced_precision(grad),)
reduced_precision.defvjp(low_keep, low_pass)
reduced_precision_backward.defvjp(back_keep, back_low)
EPSILON = 1e-05
ROPE_BASE = 500000.0

def matrix_multiply(left, right):
    return jnp.dot(left, right, precision=lax.Precision.HIGHEST, preferred_element_type=jnp.float32)

def apply_rotation(values, token_positions, head_count, direction):
    head_width = values.shape[-1] // head_count
    half_width = head_width // 2
    frequency = ROPE_BASE ** (-jnp.arange(half_width, dtype=jnp.float32) * 2.0 / head_width)
    angles = token_positions.astype(jnp.float32)[:, None] * frequency[None, :]
    cosine = jnp.cos(angles)[:, None, :]
    sine_part = direction * jnp.sin(angles)[:, None, :]
    shaped = values.reshape(values.shape[0], head_count, head_width)
    first_half = shaped[..., :half_width]
    second_half = shaped[..., half_width:]
    turned = jnp.concatenate([first_half * cosine - second_half * sine_part, second_half * cosine + first_half * sine_part], axis=-1)
    return turned.reshape(values.shape)

def rms_scale(values, gain):
    scale = lax.rsqrt(lax.optimization_barrier(jnp.mean(values * values, axis=-1, keepdims=True)) + EPSILON)
    return values * scale * gain

def attend_head(stacked, allowed):
    query_rows_all, key_rows, value_rows = stacked
    scores = jnp.einsum('brqd,bsd->brqs', query_rows_all, key_rows, precision=lax.Precision.HIGHEST) * 0.125
    scores = reduced_precision_backward(scores)
    scores = jnp.where(allowed, scores, -1e+30)
    weights = reduced_precision(jax.nn.softmax(scores, axis=-1))
    return jnp.einsum('brqs,bsd->brqd', weights, value_rows, precision=lax.Precision.HIGHEST)

def block_forward(prompt_vals, cont_vals, gain_attn, gain_ffn, router, w_query, key_projection, w_value, w_out, w_gate, w_up, w_down, prompt_mask, cont_mask, shard_apply, cont_start):
    group_number = prompt_vals.shape[0]
    continuation_count = cont_vals.shape[0]
    group_width = QUERY_HEAD_COUNT // KEY_VALUE_HEADS
    split_position = group_number * PROMPT_LENGTH
    flat_rows = jnp.concatenate([prompt_vals.reshape(-1, D), cont_vals.reshape(-1, D)], axis=0)
    prompt_pos = jnp.tile(jnp.arange(PROMPT_LENGTH, dtype=jnp.int32), group_number)
    cont_pos = (cont_start[:, None] + jnp.arange(CONTINUATION_LEN, dtype=jnp.int32)[None, :]).reshape(-1)
    token_positions = jnp.concatenate([prompt_pos, cont_pos], axis=0)
    gates_on = jnp.concatenate([prompt_mask.reshape(-1), cont_mask.reshape(-1)], axis=0).astype(jnp.float32)
    normalized_input = reduced_precision(rms_scale(flat_rows, gain_attn))
    query_rows_all = reduced_precision(apply_rotation(reduced_precision_backward(matrix_multiply(normalized_input, w_query)), token_positions, QUERY_HEAD_COUNT, 1.0))
    keys_combined = reduced_precision(apply_rotation(reduced_precision_backward(matrix_multiply(normalized_input, key_projection)), token_positions, KEY_VALUE_HEADS, 1.0))
    values_combined = reduced_precision(reduced_precision_backward(matrix_multiply(normalized_input, w_value)))
    prompt_query_rows = query_rows_all[:split_position].reshape(group_number, PROMPT_LENGTH, KEY_VALUE_HEADS, group_width, HEAD_SIZE).transpose(2, 0, 3, 1, 4)
    prompt_key_rows = keys_combined[:split_position].reshape(group_number, PROMPT_LENGTH, KEY_VALUE_HEADS, HEAD_SIZE)
    prompt_value_rows = values_combined[:split_position].reshape(group_number, PROMPT_LENGTH, KEY_VALUE_HEADS, HEAD_SIZE)
    causal = jnp.arange(PROMPT_LENGTH)[None, :] <= jnp.arange(PROMPT_LENGTH)[:, None]
    prompt_o = lax.map(jax.checkpoint(partial(attend_head, allowed=causal)), (prompt_query_rows, prompt_key_rows.transpose(2, 0, 1, 3), prompt_value_rows.transpose(2, 0, 1, 3)))
    prompt_o = prompt_o.transpose(1, 3, 0, 2, 4).reshape(split_position, QUERY_HEAD_COUNT * HEAD_SIZE)
    continuation_query = query_rows_all[split_position:].reshape(continuation_count, CONTINUATION_LEN, KEY_VALUE_HEADS, group_width, HEAD_SIZE).transpose(2, 0, 3, 1, 4)
    continuation_keys = jnp.concatenate([prompt_key_rows[shard_apply], keys_combined[split_position:].reshape(continuation_count, CONTINUATION_LEN, KEY_VALUE_HEADS, HEAD_SIZE)], axis=1)
    continuation_values = jnp.concatenate([prompt_value_rows[shard_apply], values_combined[split_position:].reshape(continuation_count, CONTINUATION_LEN, KEY_VALUE_HEADS, HEAD_SIZE)], axis=1)
    allowed_cont = jnp.concatenate([jnp.ones((CONTINUATION_LEN, PROMPT_LENGTH), dtype=bool), jnp.arange(CONTINUATION_LEN)[None, :] <= jnp.arange(CONTINUATION_LEN)[:, None]], axis=1)
    cont_o = lax.map(jax.checkpoint(partial(attend_head, allowed=allowed_cont)), (continuation_query, continuation_keys.transpose(2, 0, 1, 3), continuation_values.transpose(2, 0, 1, 3)))
    cont_o = cont_o.transpose(1, 3, 0, 2, 4).reshape(continuation_count * CONTINUATION_LEN, QUERY_HEAD_COUNT * HEAD_SIZE)
    attended = reduced_precision(reduced_precision_backward(jnp.concatenate([prompt_o, cont_o], axis=0)))
    branch_attn = reduced_precision_backward(matrix_multiply(attended, w_out))
    hidden = flat_rows + branch_attn
    normed_ffn = reduced_precision(rms_scale(hidden, gain_ffn))
    gate_pre = reduced_precision_backward(matrix_multiply(normed_ffn, w_gate))
    up_pre = reduced_precision_backward(matrix_multiply(normed_ffn, w_up))
    inner_act = reduced_precision(jax.nn.silu(gate_pre) * up_pre)
    branch_ffn = reduced_precision_backward(matrix_multiply(inner_act, w_down))
    router_gate = jax.nn.sigmoid(jnp.dot(flat_rows, router, precision=lax.Precision.HIGHEST))
    return flat_rows + (gates_on * router_gate)[:, None] * (branch_attn + branch_ffn)

def reference(prompt_in, cont_in, prompt_mask, cont_mask, cont_prompt, cont_start, gain_attn, gain_ffn, router, w_query, key_projection, w_value, w_out, w_gate, w_up, w_down, prompt_cot, cont_cot):
    params = (gain_attn.astype(jnp.float32), gain_ffn.astype(jnp.float32), router.astype(jnp.float32), w_query.astype(jnp.float32), key_projection.astype(jnp.float32), w_value.astype(jnp.float32), w_out.astype(jnp.float32), w_gate.astype(jnp.float32), w_up.astype(jnp.float32), w_down.astype(jnp.float32))
    prompt_blocks = prompt_in.astype(jnp.float32).reshape(N_FSDP, G_DEV, PROMPT_LENGTH, D)
    cont_blocks = cont_in.astype(jnp.float32).reshape(N_FSDP, CONT_BLOCK, CONTINUATION_LEN, D)
    prompt_cots = prompt_cot.astype(jnp.float32).reshape(N_FSDP, G_DEV, PROMPT_LENGTH, D)
    cont_cots = cont_cot.astype(jnp.float32).reshape(N_FSDP, CONT_BLOCK, CONTINUATION_LEN, D)
    prompt_masks = prompt_mask.reshape(N_FSDP, G_DEV, PROMPT_LENGTH)
    cont_masks = cont_mask.reshape(N_FSDP, CONT_BLOCK, CONTINUATION_LEN)
    local_maps = cont_prompt.reshape(N_FSDP, CONT_BLOCK) - (jnp.arange(N_FSDP, dtype=jnp.int32) * G_DEV)[:, None]
    starts = cont_start.reshape(N_FSDP, CONT_BLOCK)

    def block_step(totals, inputs):
        prompt_vals, cont_vals, prompt_m, cont_m, shard_apply, start_pos, prompt_c, cont_c = inputs

        def forward(prompt_arg, cont_arg, *weights):
            return block_forward(prompt_arg, cont_arg, *weights, prompt_m, cont_m, shard_apply, start_pos)
        result, pullback = jax.vjp(forward, prompt_vals, cont_vals, *params)
        cotangent = jnp.concatenate([prompt_c.reshape(-1, D), cont_c.reshape(-1, D)], axis=0)
        gradients = pullback(cotangent)
        new_totals = jax.tree.map(jnp.add, totals, tuple(gradients[2:]))
        split_position = G_DEV * PROMPT_LENGTH
        outputs = (result[:split_position].reshape(G_DEV, PROMPT_LENGTH, D), result[split_position:].reshape(CONT_BLOCK, CONTINUATION_LEN, D), gradients[0], gradients[1])
        return (new_totals, outputs)
    zero_grads = tuple((jnp.zeros_like(weight) for weight in params))
    totals, stacked = lax.scan(block_step, zero_grads, (prompt_blocks, cont_blocks, prompt_masks, cont_masks, local_maps, starts, prompt_cots, cont_cots))
    prompt_out = stacked[0].reshape(GROUPS, PROMPT_LENGTH, D).astype(jnp.bfloat16)
    cont_out = stacked[1].reshape(CONTS, CONTINUATION_LEN, D).astype(jnp.bfloat16)
    prompt_grad = stacked[2].reshape(GROUPS, PROMPT_LENGTH, D)
    cont_grad = stacked[3].reshape(CONTS, CONTINUATION_LEN, D)
    return (prompt_out, cont_out, prompt_grad, cont_grad, totals[0], totals[1], totals[2], totals[3], totals[4], totals[5], totals[6], totals[7], totals[8], totals[9])
```

```python
import jax
import jax.numpy as jnp
from jax import lax
from jax.sharding import PartitionSpec as P

HEAD_SIZE = 64
CONTINUATION_LEN = 128
EPSILON = 1e-05
ROPE_BASE = 500000.0
BF = jnp.bfloat16
F32 = jnp.float32
EVERY = ("fsdp", "ctx")


def product(left, right):
    return jnp.dot(left, right, preferred_element_type=F32)


def product_nt(left, right):
    return lax.dot_general(left, right, (((1,), (1,)), ((), ())), preferred_element_type=F32)


def product_tn(left, right):
    return lax.dot_general(left, right, (((0,), (0,)), ((), ())), preferred_element_type=F32)


def swap(value, axis, step):
    count = lax.axis_size(axis)
    return lax.ppermute(value, axis, [(i, i ^ step) for i in range(count)])


def pieces_of(value, axis="tp"):
    return [value] + [swap(value, axis, step) for step in range(1, lax.axis_size(axis))]


def all_sum(value, axis="tp"):
    parts = pieces_of(value, axis)
    total = parts[0]
    for part in parts[1:]:
        total = total + part
    return total


def lay_out(parts, width):
    me = lax.axis_index("tp")
    rows = parts[0].shape[0]
    whole = jnp.zeros((rows, width * len(parts)), parts[0].dtype)
    for step, part in enumerate(parts):
        whole = lax.dynamic_update_slice(whole, part, (0, (me ^ step) * width))
    return whole


def scatter_sum(make_block):
    me = lax.axis_index("tp")
    total = make_block(me)
    for step in range(1, lax.axis_size("tp")):
        total = total + swap(make_block(me ^ step).astype(BF), "tp", step).astype(F32)
    return total


def columns(matrix, block, width):
    return lax.dynamic_slice(matrix, (0, block * width), (matrix.shape[0], width))


def rows_of(matrix, block, width):
    return lax.dynamic_slice(matrix, (block * width, 0), (width, matrix.shape[1]))


def rope_tables(positions):
    half = HEAD_SIZE // 2
    frequency = ROPE_BASE ** (-jnp.arange(half, dtype=F32) * 2.0 / HEAD_SIZE)
    angles = positions.astype(F32)[:, None] * frequency[None, :]
    return jnp.cos(angles), jnp.sin(angles)


def rotate(values, tables, direction):
    half = HEAD_SIZE // 2
    cosine = tables[0][:, None, :]
    sine = direction * tables[1][:, None, :]
    shaped = values.reshape(values.shape[0], -1, HEAD_SIZE)
    first, second = shaped[..., :half], shaped[..., half:]
    turned = jnp.concatenate([first * cosine - second * sine, second * cosine + first * sine], -1)
    return turned.reshape(values.shape)


def attend_scores(query_split, key_split, allowed):
    scores = (
        jnp.einsum("gqkrd,gskd->gkrqs", query_split, key_split, preferred_element_type=F32) * 0.125
    )
    return jnp.where(allowed, scores, -1e30)


def attend_forward(query_split, key_split, value_split, allowed):
    scores = attend_scores(query_split, key_split, allowed)
    row_max = jnp.max(scores, axis=-1, keepdims=True)
    exponent = jnp.exp(scores - row_max)
    total = jnp.sum(exponent, axis=-1, keepdims=True)
    prob_low = (exponent / total).astype(BF)
    result = jnp.einsum(
        "gkrqs,gskd->gqkrd", prob_low, value_split, preferred_element_type=F32
    ).astype(BF)
    return result.reshape(result.shape[0] * result.shape[1], -1), row_max + jnp.log(total)


def attend_backward(query_split, key_split, value_split, allowed, log_total, out_grad):
    grad_split = out_grad.reshape(query_split.shape)
    scores = attend_scores(query_split, key_split, allowed)
    prob_full = jnp.exp(scores - log_total)
    prob_low = prob_full.astype(BF)
    value_grad = jnp.einsum("gkrqs,gqkrd->gskd", prob_low, grad_split, preferred_element_type=F32)
    prob_grad = jnp.einsum("gqkrd,gskd->gkrqs", grad_split, value_split, preferred_element_type=F32)
    score_grad = (
        prob_full * (prob_grad - jnp.sum(prob_grad * prob_full, axis=-1, keepdims=True))
    ).astype(BF)
    query_grad = (
        jnp.einsum("gkrqs,gskd->gqkrd", score_grad, key_split, preferred_element_type=F32) * 0.125
    )
    key_grad = (
        jnp.einsum("gkrqs,gqkrd->gskd", score_grad, query_split, preferred_element_type=F32) * 0.125
    )
    batch = query_split.shape[0]
    return (
        query_grad.reshape(batch * query_split.shape[1], -1),
        key_grad.reshape(batch, key_split.shape[1], -1),
        value_grad.reshape(batch, key_split.shape[1], -1),
    )


def body(
    prompt_in,
    cont_in,
    prompt_mask,
    cont_mask,
    cont_prompt,
    cont_start,
    gain_attn,
    gain_ffn,
    router,
    w_query,
    key_projection,
    w_value,
    w_out,
    w_gate,
    w_up,
    w_down,
    prompt_cot,
    cont_cot,
):
    groups, prompt_rows, width = prompt_in.shape
    conts = cont_in.shape[0]
    tp_size = lax.axis_size("tp")
    ctx_size = lax.axis_size("ctx")
    model_width = width * tp_size
    me_tp = lax.axis_index("tp")
    me_ctx = lax.axis_index("ctx")
    query_width = w_query.shape[1]
    key_width = key_projection.shape[1]
    query_heads = query_width // HEAD_SIZE
    key_heads = key_width // HEAD_SIZE
    ratio = query_heads // key_heads
    tokens_in = [prompt_in.reshape(-1, width), cont_in.reshape(-1, width)]
    cots = [prompt_cot.reshape(-1, width), cont_cot.reshape(-1, width)]
    masks = [prompt_mask.reshape(-1).astype(F32), cont_mask.reshape(-1).astype(F32)]
    prompt_place = me_ctx * prompt_rows + jnp.arange(prompt_rows, dtype=jnp.int32)
    cont_place = (
        cont_start[:, None] + jnp.arange(CONTINUATION_LEN, dtype=jnp.int32)[None, :]
    ).reshape(-1)
    tables = [rope_tables(jnp.tile(prompt_place, groups)), rope_tables(cont_place)]
    local_prompt = cont_prompt - lax.axis_index("fsdp") * groups

    def quarter_rows(weight):
        rows = weight.shape[0] // ctx_size
        return lax.dynamic_slice(weight, (me_ctx * rows, 0), (rows, weight.shape[1]))

    def quarter_columns(weight):
        count = weight.shape[1] // ctx_size
        return lax.dynamic_slice(weight, (0, me_ctx * count), (weight.shape[0], count))

    full_qkv = lax.all_gather(
        jnp.concatenate(
            [quarter_rows(w_query), quarter_rows(key_projection), quarter_rows(w_value)], axis=1
        ),
        EVERY,
        axis=0,
        tiled=True,
    )
    full_out = lax.all_gather(quarter_columns(w_out), EVERY, axis=1, tiled=True)
    full_gate = lax.all_gather(quarter_rows(w_gate), EVERY, axis=0, tiled=True)
    full_up = lax.all_gather(quarter_rows(w_up), EVERY, axis=0, tiled=True)
    full_down = lax.all_gather(quarter_columns(w_down), EVERY, axis=1, tiled=True)

    params = [p.astype(F32) for p in pieces_of(jnp.stack([gain_attn, gain_ffn, router]))]
    gains_attn = [p[0] for p in params]
    gains_ffn = [p[1] for p in params]
    routers = [p[2] for p in params]
    x_parts = [pieces_of(t) for t in tokens_in]
    cot_parts = [pieces_of(t) for t in cots]
    streams = range(2)

    scale_attn, gate_router, mixing, xn1 = [], [], [], []
    for i in streams:
        wide = [p.astype(F32) for p in x_parts[i]]
        squares = sum(jnp.sum(p * p, axis=1) for p in wide)
        logits = sum(jnp.sum(p * r, axis=1) for p, r in zip(wide, routers))
        scale = lax.rsqrt(squares / model_width + EPSILON)
        gate = jax.nn.sigmoid(logits)
        scale_attn.append(scale)
        gate_router.append(gate)
        mixing.append(masks[i] * gate)
        xn1.append(
            lay_out([(p * scale[:, None] * g).astype(BF) for p, g in zip(wide, gains_attn)], width)
        )
    qkv = [product(t, full_qkv) for t in xn1]
    query = [rotate(t[:, :query_width], tb, 1.0).astype(BF) for t, tb in zip(qkv, tables)]
    key = [
        rotate(t[:, query_width : query_width + key_width], tb, 1.0).astype(BF)
        for t, tb in zip(qkv, tables)
    ]
    value = [t[:, query_width + key_width :].astype(BF) for t in qkv]

    own_kv = jnp.concatenate([key[0], value[0]], axis=1).reshape(groups, prompt_rows, 2 * key_width)
    prompt_kv = jnp.zeros((groups, prompt_rows * ctx_size, 2 * key_width), BF)
    for step, part in enumerate(pieces_of(own_kv, "ctx")):
        prompt_kv = lax.dynamic_update_slice(prompt_kv, part, (0, (me_ctx ^ step) * prompt_rows, 0))
    length = prompt_rows * ctx_size
    prompt_k, prompt_v = prompt_kv[..., :key_width], prompt_kv[..., key_width:]

    def heads(t, batch):
        return t.reshape(batch, -1, key_heads, HEAD_SIZE)

    all_query = [
        query[0].reshape(groups, prompt_rows, key_heads, ratio, HEAD_SIZE),
        query[1].reshape(conts, CONTINUATION_LEN, key_heads, ratio, HEAD_SIZE),
    ]
    all_key = [
        heads(prompt_k, groups),
        jnp.concatenate(
            [
                heads(jnp.take(prompt_k, local_prompt, axis=0), conts),
                heads(key[1], conts),
            ],
            axis=1,
        ),
    ]
    all_value = [
        heads(prompt_v, groups),
        jnp.concatenate(
            [
                heads(jnp.take(prompt_v, local_prompt, axis=0), conts),
                heads(value[1], conts),
            ],
            axis=1,
        ),
    ]
    allowed = [
        jnp.arange(length, dtype=jnp.int32)[None, :] <= prompt_place[:, None],
        jnp.concatenate(
            [
                jnp.ones((CONTINUATION_LEN, length), dtype=bool),
                jnp.arange(CONTINUATION_LEN)[None, :] <= jnp.arange(CONTINUATION_LEN)[:, None],
            ],
            axis=1,
        ),
    ]
    attended, log_total = [], []
    for i in streams:
        result, total = attend_forward(all_query[i], all_key[i], all_value[i], allowed[i])
        attended.append(result)
        log_total.append(total)

    branch_attn = [
        scatter_sum(lambda b, t=t: product(t, columns(full_out, b, width))) for t in attended
    ]
    a_parts = [pieces_of(a.astype(BF)) for a in branch_attn]
    scale_ffn, xn2, hidden_parts = [], [], []
    for i in streams:
        hid = [x.astype(F32) + a.astype(F32) for x, a in zip(x_parts[i], a_parts[i])]
        scale = lax.rsqrt(sum(jnp.sum(h * h, axis=1) for h in hid) / model_width + EPSILON)
        scale_ffn.append(scale)
        hidden_parts.append(hid)
        xn2.append(
            lay_out([(h * scale[:, None] * g).astype(BF) for h, g in zip(hid, gains_ffn)], width)
        )
    grad_parts = [[c.astype(F32) * mixing[i][:, None] for c in cot_parts[i]] for i in streams]
    ffn_grad = [lay_out([g.astype(BF) for g in grad_parts[i]], width) for i in streams]

    inner, gate_grad, up_grad = [], [], []
    for i in streams:
        g = product(xn2[i], full_gate)
        u = product(xn2[i], full_up)
        s = jax.nn.sigmoid(g)
        inner.append((g * s * u).astype(BF))
        dz = product_nt(ffn_grad[i], full_down)
        gate_grad.append((dz * u * s * (1.0 + g * (1.0 - s))).astype(BF))
        up_grad.append((dz * g * s).astype(BF))

    normed_grad = [
        scatter_sum(
            lambda b, i=i: product_nt(gate_grad[i], rows_of(full_gate, b, width))
            + product_nt(up_grad[i], rows_of(full_up, b, width))
        )
        for i in streams
    ]
    n_parts = [pieces_of(n.astype(BF)) for n in normed_grad]
    back_ffn, dab, gain_ffn_sum = [], [], 0.0
    for i in streams:
        wide = [n.astype(F32) for n in n_parts[i]]
        hid = hidden_parts[i]
        total = sum(jnp.sum(h * g * n, axis=1) for h, g, n in zip(hid, gains_ffn, wide))
        scale = scale_ffn[i]
        factor = (scale**3 * total / model_width)[:, None]
        parts = [
            (d + scale[:, None] * g * n - h * factor).astype(BF)
            for d, g, n, h in zip(grad_parts[i], gains_ffn, wide, hid)
        ]
        dab.append(lay_out(parts, width))
        hid_own = tokens_in[i].astype(F32) + branch_attn[i]
        back_ffn.append(scale[:, None] * gains_ffn[0] * normed_grad[i] - hid_own * factor)
        gain_ffn_sum = gain_ffn_sum + jnp.sum(hid_own * scale[:, None] * normed_grad[i], axis=0)

    branch_ffn = [
        scatter_sum(lambda b, t=t: product(t, columns(full_down, b, width))) for t in inner
    ]
    both = lambda pair: jnp.concatenate(pair, axis=0)

    def reduce_rows(partial_grad):
        part = lax.psum_scatter(partial_grad.astype(BF), EVERY, scatter_dimension=0, tiled=True)
        return lax.all_gather(part, "ctx", axis=0, tiled=True).astype(F32)

    def reduce_columns(partial_grad):
        part = lax.psum_scatter(partial_grad.astype(BF), EVERY, scatter_dimension=1, tiled=True)
        return lax.all_gather(part, "ctx", axis=1, tiled=True).astype(F32)

    grad_down = reduce_columns(product_tn(both(inner), both(ffn_grad)))
    xn2_all = both(xn2)
    grad_gate = reduce_rows(product_tn(xn2_all, both(gate_grad)))
    grad_up = reduce_rows(product_tn(xn2_all, both(up_grad)))

    do = [product_nt(t, full_out).astype(BF) for t in dab]
    grad_out = reduce_columns(product_tn(both(attended), both(dab)))
    back = [
        attend_backward(all_query[i], all_key[i], all_value[i], allowed[i], log_total[i], do[i])
        for i in streams
    ]
    one_hot = (local_prompt[:, None] == jnp.arange(groups, dtype=jnp.int32)[None, :]).astype(F32)
    kv_grad = jnp.concatenate(
        [
            back[0][j]
            + jnp.einsum(
                "cg,csx->gsx",
                one_hot,
                back[1][j][:, :length],
                precision=lax.Precision.HIGHEST,
            )
            for j in (1, 2)
        ],
        axis=2,
    )

    def ctx_block(step):
        return lax.dynamic_slice(
            kv_grad, (0, (me_ctx ^ step) * prompt_rows, 0), (groups, prompt_rows, 2 * key_width)
        )

    kv_mine = ctx_block(0)
    for step in range(1, ctx_size):
        kv_mine = kv_mine + swap(ctx_block(step).astype(BF), "ctx", step).astype(F32)
    dk = [
        kv_mine[..., :key_width].reshape(-1, key_width),
        back[1][1][:, length:].reshape(-1, key_width),
    ]
    dv = [
        kv_mine[..., key_width:].reshape(-1, key_width),
        back[1][2][:, length:].reshape(-1, key_width),
    ]
    dq = [back[0][0], back[1][0]]
    dqkv, total_attn = [], []
    for i in streams:
        dqkv.append(
            jnp.concatenate(
                [
                    rotate(dq[i], tables[i], -1.0).astype(BF),
                    rotate(dk[i], tables[i], -1.0).astype(BF),
                    dv[i].astype(BF),
                ],
                axis=1,
            )
        )
        total_attn.append(
            all_sum(
                jnp.sum(dq[i] * query[i].astype(F32), axis=1)
                + jnp.sum(dk[i] * key[i].astype(F32), axis=1)
                + jnp.sum(dv[i] * value[i].astype(F32), axis=1)
            )
        )
    grad_qkv = reduce_rows(product_tn(both(xn1), both(dqkv)))
    normed_attn_grad = [
        scatter_sum(lambda b, t=t: product_nt(t, rows_of(full_qkv, b, width))) for t in dqkv
    ]

    gain_attn_sum, router_sum = 0.0, 0.0
    outs, token_grads = [], []
    for i in streams:
        x = tokens_in[i].astype(F32)
        dy = cots[i].astype(F32)
        branch = branch_attn[i] + branch_ffn[i]
        outs.append((x + mixing[i][:, None] * branch).astype(BF))
        dl = (1.0 - gate_router[i]) * all_sum(jnp.sum(grad_parts[i][0] * branch, axis=1))
        router_sum = router_sum + jnp.sum(x * dl[:, None], axis=0)
        scale = scale_attn[i]
        n = normed_attn_grad[i]
        gain_attn_sum = gain_attn_sum + jnp.sum(x * scale[:, None] * n, axis=0)
        n1 = (
            scale[:, None] * gains_attn[0] * n
            - x * (scale**2 * total_attn[i] / model_width)[:, None]
        )
        token_grads.append(dy + dl[:, None] * routers[0] + back_ffn[i] + n1)
    small = lax.psum((gain_attn_sum, gain_ffn_sum, router_sum), EVERY)
    return (
        outs[0].reshape(prompt_in.shape),
        outs[1].reshape(cont_in.shape),
        token_grads[0].reshape(prompt_in.shape),
        token_grads[1].reshape(cont_in.shape),
        small[0],
        small[1],
        small[2],
        grad_qkv[:, :query_width],
        grad_qkv[:, query_width : query_width + key_width],
        grad_qkv[:, query_width + key_width :],
        grad_out,
        grad_gate,
        grad_up,
        grad_down,
    )


def solution(mesh):
    placed = (
        P("fsdp", "ctx", "tp"),
        P(("fsdp", "ctx"), None, "tp"),
        P("fsdp", "ctx"),
        P(("fsdp", "ctx"), None),
        P(("fsdp", "ctx")),
        P(("fsdp", "ctx")),
        P("tp"),
        P("tp"),
        P("tp"),
        P("fsdp", "tp"),
        P("fsdp", "tp"),
        P("fsdp", "tp"),
        P("tp", "fsdp"),
        P("fsdp", "tp"),
        P("fsdp", "tp"),
        P("tp", "fsdp"),
        P("fsdp", "ctx", "tp"),
        P(("fsdp", "ctx"), None, "tp"),
    )
    return jax.shard_map(
        body,
        mesh=mesh,
        in_specs=placed,
        out_specs=(
            P("fsdp", "ctx", "tp"),
            P(("fsdp", "ctx"), None, "tp"),
            P("fsdp", "ctx", "tp"),
            P(("fsdp", "ctx"), None, "tp"),
            P("tp"),
            P("tp"),
            P("tp"),
            P("fsdp", "tp"),
            P("fsdp", "tp"),
            P("fsdp", "tp"),
            P("tp", "fsdp"),
            P("fsdp", "tp"),
            P("fsdp", "tp"),
            P("tp", "fsdp"),
        ),
        check_vma=False,
    )
```

```python
import functools

import jax
import jax.numpy as jnp
from jax import lax
from jax.experimental import pallas as pl
from jax.experimental.pallas import tpu as pltpu
from jax.sharding import PartitionSpec as P

HEAD_SIZE = 64
CONTINUATION_LEN = 128
EPSILON = 1e-05
ROPE_BASE = 500000.0
BF = jnp.bfloat16
F32 = jnp.float32
EVERY = ("fsdp", "ctx")


def product(left, right):
    return jnp.dot(left, right, preferred_element_type=F32)


def product_nt(left, right):
    return lax.dot_general(left, right, (((1,), (1,)), ((), ())), preferred_element_type=F32)


def product_tn(left, right):
    return lax.dot_general(left, right, (((0,), (0,)), ((), ())), preferred_element_type=F32)


def swap(value, axis, step):
    count = lax.axis_size(axis)
    return lax.ppermute(value, axis, [(i, i ^ step) for i in range(count)])


def pieces_of(value, axis="tp"):
    return [value] + [swap(value, axis, step) for step in range(1, lax.axis_size(axis))]


def tie(values, deps):
    return lax.optimization_barrier((values, deps))[0]


def inner_pair():
    me = lax.axis_index("tp")
    return (me == 1) | (me == 2)


def gather_tp(value):
    if lax.axis_size("tp") != 4:
        parts = pieces_of(value)
        return parts, parts[1:]
    second = swap(value, "tp", 2)
    first = swap(value, "tp", 1)
    middle = lax.ppermute(value, "tp", [(1, 2), (2, 1)])
    passed = lax.ppermute(second, "tp", [(2, 3), (1, 0)])
    third = jnp.where(inner_pair(), middle, passed)
    return [value, first, second, third], [first, second, middle]


def all_sum(value, axis="tp"):
    parts = pieces_of(value, axis)
    total = parts[0]
    for part in parts[1:]:
        total = total + part
    return total


def group_sum(value):
    if not paired():
        return lax.psum(value, EVERY)
    for axis, step in (("ctx", 1), ("ctx", 2), ("fsdp", 1)):
        value = value + swap(value, axis, step)
    return value


def blocks_of(make_block):
    me = lax.axis_index("tp")
    blocks = [make_block(me ^ step) for step in range(lax.axis_size("tp"))]
    if len(blocks) != 4:
        return [blocks[0]] + [block.astype(BF) for block in blocks[1:]]
    return [blocks[0], blocks[1].astype(BF), blocks[2], blocks[3].astype(BF)]


def exchange_sum(blocks):
    if len(blocks) != 4:
        sent = [swap(block, "tp", step) for step, block in enumerate(blocks) if step > 0]
    else:
        passed = lax.ppermute(blocks[3], "tp", [(3, 2), (0, 1)])
        middle = lax.ppermute(blocks[3], "tp", [(1, 2), (2, 1)])
        first = swap(blocks[1], "tp", 1)
        relay = (blocks[2] + passed.astype(F32)).astype(BF)
        sent = [middle, first, swap(relay, "tp", 2)]
    total = blocks[0]
    for part in sent:
        total = total + part.astype(F32)
    return total


def columns(matrix, block, width):
    return lax.dynamic_slice(matrix, (0, block * width), (matrix.shape[0], width))


def rows_of(matrix, block, width):
    return lax.dynamic_slice(matrix, (block * width, 0), (width, matrix.shape[1]))


def cut_of(matrix, axis, block, width):
    return rows_of(matrix, block, width) if axis == 0 else columns(matrix, block, width)


def paired():
    return lax.axis_size("fsdp") == 2 and lax.axis_size("ctx") == 4


def gather_weight(weight, axis, after=None):
    me = lax.axis_index("ctx")
    size = weight.shape[axis] // lax.axis_size("ctx")
    quarter = cut_of(weight, axis, me, size)
    if not paired():
        return lax.all_gather(quarter, EVERY, axis=axis, tiled=True), quarter
    if after is not None:
        quarter = tie(quarter, after)
    mine = lax.axis_index("fsdp")
    far = swap(quarter, "fsdp", 1)
    across = swap(far, "ctx", 2)
    found = [(0, far), (2, across), (1, swap(far, "ctx", 1)), (3, swap(across, "ctx", 1))]
    shape = list(weight.shape)
    shape[axis] *= 2
    whole = jnp.zeros(shape, weight.dtype)

    def put(whole, part, start):
        return lax.dynamic_update_slice(whole, part, (start, 0) if axis == 0 else (0, start))

    whole = put(whole, weight, mine * size * 4)
    for step, part in found:
        whole = put(whole, part, ((1 - mine) * 4 + (me ^ step)) * size)
    return whole, far


def gather_weight_offload(weight, axis, after):
    size = weight.shape[axis] // lax.axis_size("ctx")
    quarter = tie(cut_of(weight, axis, lax.axis_index("ctx"), size), after)
    return lax.all_gather(quarter, EVERY, axis=axis, tiled=True)


def gather_out(weight):
    if not paired():
        pieces, done = gather_tp(lax.all_gather(weight, "fsdp", axis=1, tiled=True))
        return jnp.concatenate(pieces, axis=0), done
    me = lax.axis_index("ctx")
    mine = lax.axis_index("fsdp")
    size = weight.shape[1] // lax.axis_size("ctx")
    pieces, done = gather_tp(columns(weight, me, size))
    own = jnp.concatenate(pieces, axis=0)
    far = swap(own, "fsdp", 1)
    found = [(mine, 0, own), (1 - mine, 0, far)]
    found += [(mine, 2, swap(own, "ctx", 2)), (1 - mine, 2, swap(far, "ctx", 2))]
    found += [(f, step ^ 1, swap(part, "ctx", 1)) for f, step, part in found]
    whole = jnp.zeros((own.shape[0], size * 8), weight.dtype)
    for f, step, part in found:
        whole = lax.dynamic_update_slice(whole, part, (0, (f * 4 + (me ^ step)) * size))
    return whole, done


def grad_start(left, right, axis):
    if not paired():
        whole = product_tn(left, right).astype(BF)
        return whole, whole, whole
    mine = lax.axis_index("fsdp")
    core = lax.axis_index("ctx") % 2
    split, other = (left, right) if axis == 0 else (right, left)
    half = lambda m, i: columns(m, i, m.shape[1] // 2)
    split_far, split_own = half(split, 1 - mine), half(split, mine)
    other_far, other_own = half(other, 1 - core), half(other, core)
    dot = lambda s, t: product_tn(s, t) if axis == 0 else product_tn(t, s)
    first = swap(dot(split_far, other_far).astype(BF), "ctx", 1)
    second = swap(dot(split_own, other_far).astype(BF), "ctx", 1)
    far = (dot(split_far, other_own) + first.astype(F32)).astype(BF)
    kept = dot(split_own, other_own) + second.astype(F32)
    return swap(far, "fsdp", 1), kept, far


def grad_middle(arrived, kept, far, axis):
    if not paired():
        return lax.psum_scatter(kept, EVERY, scatter_dimension=axis, tiled=True)
    side = lax.axis_index("ctx") // 2
    size = kept.shape[axis] // 2
    half = lambda i: cut_of(kept, axis, i, size) + cut_of(arrived, axis, i, size).astype(F32)
    sent = swap(half(1 - side).astype(BF), "ctx", 2)
    return (half(side) + sent.astype(F32)).astype(BF)


def grad_end(piece, axis):
    if not paired():
        return lax.all_gather(piece, "ctx", axis=axis, tiled=True).astype(F32)
    side = lax.axis_index("ctx") // 2
    core = lax.axis_index("ctx") % 2
    across = swap(piece, "ctx", 2)
    own = in_order(piece, across, side, axis)
    return in_order(own, swap(own, "ctx", 1), core, 1 - axis).astype(F32)


def in_order(mine, theirs, index, axis):
    low = index == 0
    return jnp.concatenate(
        [jnp.where(low, mine, theirs), jnp.where(low, theirs, mine)], axis=axis
    )


LOG2E = 1.4426950408889634
SCORE_SCALE = 0.125
LANES = 128


def lane_index(shape):
    return lax.broadcasted_iota(jnp.int32, shape, len(shape) - 1)


def turn(tile, cosine, sine):
    low = lane_index(tile.shape) % HEAD_SIZE < HEAD_SIZE // 2
    other = jnp.where(
        low,
        pltpu.roll(tile, LANES - HEAD_SIZE // 2, 1),
        pltpu.roll(tile, HEAD_SIZE // 2, 1),
    )
    return tile * cosine + other * sine


def doubled(tile, head):
    wide = tile.astype(F32)
    low = lane_index(tile.shape) < HEAD_SIZE
    other = pltpu.roll(wide, HEAD_SIZE, 1)
    return jnp.where(low == (head == 0), wide, other).astype(tile.dtype)


def half_of(tile, j):
    low = lane_index(tile.shape) < HEAD_SIZE
    keep = low if j == 0 else jnp.logical_not(low)
    return jnp.where(keep, tile, jnp.zeros_like(tile))


def dot_nt(left, right):
    return lax.dot_general(left, right, (((1,), (1,)), ((), ())), preferred_element_type=F32)


def dot_nn(left, right):
    return lax.dot_general(left, right, (((1,), (0,)), ((), ())), preferred_element_type=F32)


def params_of(*semantics, limit=56 << 20):
    return pltpu.CompilerParams(dimension_semantics=semantics, vmem_limit_bytes=limit)


def entry_kernel(count, model_width, query_width, order, *refs):
    parts = refs[:count]
    gain, router, weight, mask, cosine, sine = refs[count : count + 6]
    xn_ref, query_ref, kv_ref, scale_ref, gate_ref, mix_ref = refs[count + 6 :]
    width = parts[0].shape[1]
    wide = [p[...].astype(F32) for p in parts]
    squares = sum(jnp.sum(w * w, axis=1, keepdims=True) for w in wide)
    logits = sum(
        jnp.sum(w * router[r : r + 1, :], axis=1, keepdims=True) for r, w in enumerate(wide)
    )
    scale = lax.rsqrt(squares / model_width + EPSILON)
    gate = jax.nn.sigmoid(logits)
    scale_ref[...] = scale
    gate_ref[...] = gate
    mix_ref[...] = mask[...] * gate
    total = None
    for r, w in enumerate(wide):
        normed = (w * scale * gain[r : r + 1, :]).astype(BF)
        place = pl.ds(pl.multiple_of(order[r] * width, width), width)
        xn_ref[:, place] = normed
        term = dot_nn(normed, weight[place, :])
        total = term if total is None else total + term
    for t in range(query_width // LANES):
        cut = slice(t * LANES, (t + 1) * LANES)
        query_ref[:, cut] = turn(total[:, cut], cosine[...], sine[...]).astype(BF)
    key_width = kv_ref.shape[1] // 2
    key = total[:, query_width : query_width + key_width]
    kv_ref[:, :key_width] = turn(key, cosine[...], sine[...]).astype(BF)
    kv_ref[:, key_width:] = total[:, query_width + key_width :].astype(BF)


def entry(parts, gains, routers, weight, mask, tables, order, query_width):
    rows, width = parts[0].shape
    count = len(parts)
    block = min(rows, 256)
    total_width = weight.shape[1]
    kv_width = total_width - query_width
    whole = lambda a: pl.BlockSpec(a.shape, lambda i, o: (0, 0))
    row = lambda w: pl.BlockSpec((block, w), lambda i, o: (i, 0))
    outs = [(width * count, BF), (query_width, BF), (kv_width, BF), (1, F32), (1, F32), (1, F32)]
    return pl.pallas_call(
        functools.partial(entry_kernel, count, width * count, query_width),
        out_shape=[jax.ShapeDtypeStruct((rows, w), d) for w, d in outs],
        grid_spec=pltpu.PrefetchScalarGridSpec(
            num_scalar_prefetch=1,
            grid=(rows // block,),
            in_specs=[row(width)] * count
            + [whole(gains), whole(routers), whole(weight), row(1), row(LANES), row(LANES)],
            out_specs=[row(w) for w, d in outs],
        ),
        compiler_params=params_of("arbitrary"),
        cost_estimate=pl.CostEstimate(
            flops=2 * rows * width * count * total_width,
            bytes_accessed=rows * width * count * 4 + weight.size * 2,
            transcendentals=rows,
        ),
        name="entry",
    )(order, *parts, gains, routers, weight, mask, *tables)


def softmax_columns(keys, biases, queries, scores):
    top = None
    for i, (key, bias) in enumerate(zip(keys, biases)):
        s = dot_nt(key, queries) * (SCORE_SCALE * LOG2E)
        if bias is not None:
            s = s + bias
        scores[i][...] = s
        part = jnp.max(s, axis=0, keepdims=True)
        top = part if top is None else jnp.maximum(top, part)
    total = 0.0
    for ref in scores:
        e = jnp.exp2(ref[...] - top)
        ref[...] = e
        total = total + jnp.sum(e, axis=0, keepdims=True)
    share = 1.0 / total
    return [(ref[...] * share).astype(BF) for ref in scores], top + jnp.log2(total)


def causal_bias(keys, rows, start):
    key = lax.broadcasted_iota(jnp.int32, (keys, rows), 0)
    row = lax.broadcasted_iota(jnp.int32, (keys, rows), 1)
    return jnp.where(key <= row + start, 0.0, -1e30)


def prompt_forward_kernel(start, q_ref, kv_ref, o_ref, lse_ref, vt_ref, bias_ref, s_ref):
    tile = pl.program_id(1)
    rows = q_ref.shape[1]
    head = tile // (pl.num_programs(1) // 2)

    @pl.when((pl.program_id(0) == 0) & (tile == 0))
    def _():
        bias_ref[...] = causal_bias(bias_ref.shape[0], rows, start[0])

    @pl.when(tile == 0)
    def _():
        vt_ref[...] = kv_ref[0, :, LANES:].astype(F32).T.astype(BF)

    key = doubled(kv_ref[0, :, :LANES], head)
    value_t = vt_ref[pl.ds(pl.multiple_of(head * HEAD_SIZE, HEAD_SIZE), HEAD_SIZE), :]
    query = q_ref[0]
    outs = []
    for j in range(2):
        probs, lse = softmax_columns([key], [bias_ref[...]], half_of(query, j), [s_ref])
        lse_ref[0, 0, j : j + 1, :] = lse
        outs.append(dot_nn(value_t, probs[0]))
    o_ref[0] = jnp.concatenate(outs, axis=0).T.astype(BF)


def prompt_forward(query, kv, start):
    groups, rows, query_width = query.shape
    length = kv.shape[1]
    tiles = query_width // LANES
    return pl.pallas_call(
        prompt_forward_kernel,
        out_shape=[
            jax.ShapeDtypeStruct(query.shape, BF),
            jax.ShapeDtypeStruct((groups, tiles, 2, rows), F32),
        ],
        grid_spec=pltpu.PrefetchScalarGridSpec(
            num_scalar_prefetch=1,
            grid=(groups, tiles),
            in_specs=[
                pl.BlockSpec((1, rows, LANES), lambda g, t, s: (g, 0, t)),
                pl.BlockSpec((1, length, 2 * LANES), lambda g, t, s: (g, 0, 0)),
            ],
            out_specs=[
                pl.BlockSpec((1, rows, LANES), lambda g, t, s: (g, 0, t)),
                pl.BlockSpec((1, 1, 2, rows), lambda g, t, s: (g, t, 0, 0)),
            ],
            scratch_shapes=[
                pltpu.VMEM((LANES, length), BF),
                pltpu.VMEM((length, rows), F32),
                pltpu.VMEM((length, rows), F32),
            ],
        ),
        compiler_params=params_of("arbitrary", "arbitrary"),
        cost_estimate=pl.CostEstimate(
            flops=8 * groups * tiles * rows * length * LANES,
            bytes_accessed=query.size * 4 + kv.size * 2,
            transcendentals=groups * tiles * 2 * rows * length,
        ),
        name="prompt_forward",
    )(start, query, kv)


def cont_forward_kernel(which, q_ref, kv_ref, own_ref, o_ref, lse_ref, vt_ref, wt_ref, s_ref, t_ref):
    tile = pl.program_id(1)
    rows = q_ref.shape[1]
    head = tile // (pl.num_programs(1) // 2)

    @pl.when(tile == 0)
    def _():
        vt_ref[...] = kv_ref[0, :, LANES:].astype(F32).T.astype(BF)
        wt_ref[...] = own_ref[0, :, LANES:].astype(F32).T.astype(BF)

    place = pl.ds(pl.multiple_of(head * HEAD_SIZE, HEAD_SIZE), HEAD_SIZE)
    keys = [doubled(kv_ref[0, :, :LANES], head), doubled(own_ref[0, :, :LANES], head)]
    query = q_ref[0]
    both = jnp.concatenate([half_of(query, 0), half_of(query, 1)], axis=0)
    bias = causal_bias(rows, rows, 0)
    probs, lse = softmax_columns(
        keys, [None, jnp.concatenate([bias, bias], axis=1)], both, [s_ref, t_ref]
    )
    out = dot_nn(vt_ref[place, :], probs[0]) + dot_nn(wt_ref[place, :], probs[1])
    lse_ref[0, 0] = lse
    o_ref[0] = jnp.concatenate([out[:, :rows], out[:, rows:]], axis=0).T.astype(BF)


def cont_forward(query, kv, own, which):
    conts, rows, query_width = query.shape
    length = kv.shape[1]
    tiles = query_width // LANES
    return pl.pallas_call(
        cont_forward_kernel,
        out_shape=[
            jax.ShapeDtypeStruct(query.shape, BF),
            jax.ShapeDtypeStruct((conts, tiles, 1, 2 * rows), F32),
        ],
        grid_spec=pltpu.PrefetchScalarGridSpec(
            num_scalar_prefetch=1,
            grid=(conts, tiles),
            in_specs=[
                pl.BlockSpec((1, rows, LANES), lambda g, t, w: (g, 0, t)),
                pl.BlockSpec((1, length, 2 * LANES), lambda g, t, w: (w[g], 0, 0)),
                pl.BlockSpec((1, rows, 2 * LANES), lambda g, t, w: (g, 0, 0)),
            ],
            out_specs=[
                pl.BlockSpec((1, rows, LANES), lambda g, t, w: (g, 0, t)),
                pl.BlockSpec((1, 1, 1, 2 * rows), lambda g, t, w: (g, t, 0, 0)),
            ],
            scratch_shapes=[
                pltpu.VMEM((LANES, length), BF),
                pltpu.VMEM((LANES, rows), BF),
                pltpu.VMEM((length, 2 * rows), F32),
                pltpu.VMEM((rows, 2 * rows), F32),
            ],
        ),
        compiler_params=params_of("arbitrary", "arbitrary"),
        cost_estimate=pl.CostEstimate(
            flops=8 * conts * tiles * rows * (length + rows) * LANES,
            bytes_accessed=query.size * 4 + conts * length * LANES * 4,
            transcendentals=conts * tiles * 2 * rows * (length + rows),
        ),
        name="cont_forward",
    )(which, query, kv, own)


def backward_columns(key, value, key_t, bias, query, grad, lse, delta, chunk):
    dks, dvs, dq = [], [], None
    for c in range(key.shape[0] // chunk):
        cut = slice(c * chunk, (c + 1) * chunk)
        s = dot_nt(key[cut], query) * (SCORE_SCALE * LOG2E)
        if bias is not None:
            s = s + bias[cut]
        p = jnp.exp2(s - lse)
        dp = dot_nt(value[cut], grad)
        ds = (p * (dp - delta)).astype(BF)
        dvs.append(dot_nn(p.astype(BF), grad))
        dks.append(dot_nn(ds, query))
        term = dot_nn(key_t[:, cut], ds)
        dq = term if dq is None else dq + term
    return dks, dvs, dq


def folded(parts, head):
    whole = jnp.concatenate(parts, axis=0)
    low = lane_index(whole.shape) < HEAD_SIZE
    return jnp.where(low == (head == 0), whole + pltpu.roll(whole, HEAD_SIZE, 1), 0.0)


def add_into(ref, value, first):
    @pl.when(first)
    def _():
        ref[0] = value

    @pl.when(jnp.logical_not(first))
    def _():
        ref[0] = ref[0] + value


def prompt_backward_kernel(
    start, q_ref, kv_ref, o_ref, g_ref, lse_ref, dq_ref, dk_ref, dv_ref, kt_ref, bias_ref
):
    tile = pl.program_id(1)
    rows = q_ref.shape[1]
    head = tile // (pl.num_programs(1) // 2)

    @pl.when((pl.program_id(0) == 0) & (tile == 0))
    def _():
        bias_ref[...] = causal_bias(bias_ref.shape[0], rows, start[0])

    @pl.when(tile == 0)
    def _():
        kt_ref[...] = kv_ref[0, :, :LANES].astype(F32).T.astype(BF)

    key = doubled(kv_ref[0, :, :LANES], head)
    value = doubled(kv_ref[0, :, LANES:], head)
    key_t = kt_ref[pl.ds(pl.multiple_of(head * HEAD_SIZE, HEAD_SIZE), HEAD_SIZE), :]
    query, grad = q_ref[0], g_ref[0]
    mixed = (grad.astype(F32) * o_ref[0].astype(F32)).T
    dks, dvs, dqs = None, None, []
    for j in range(2):
        delta = jnp.sum(mixed[j * HEAD_SIZE : (j + 1) * HEAD_SIZE], axis=0, keepdims=True)
        dk, dv, dq = backward_columns(
            key,
            value,
            key_t,
            bias_ref,
            half_of(query, j),
            half_of(grad, j),
            lse_ref[0, 0, j : j + 1, :],
            delta,
            256,
        )
        dks = dk if dks is None else [a + b for a, b in zip(dks, dk)]
        dvs = dv if dvs is None else [a + b for a, b in zip(dvs, dv)]
        dqs.append(dq)
    dq_ref[0] = jnp.concatenate(dqs, axis=0).T * SCORE_SCALE
    add_into(dk_ref, folded(dks, head) * SCORE_SCALE, tile == 0)
    add_into(dv_ref, folded(dvs, head), tile == 0)


def prompt_backward(query, kv, out, grad, lse, start):
    groups, rows, query_width = query.shape
    length = kv.shape[1]
    tiles = query_width // LANES
    q_spec = pl.BlockSpec((1, rows, LANES), lambda g, t, s: (g, 0, t))
    k_spec = pl.BlockSpec((1, length, LANES), lambda g, t, s: (g, 0, 0))
    return pl.pallas_call(
        prompt_backward_kernel,
        out_shape=[
            jax.ShapeDtypeStruct(query.shape, F32),
            jax.ShapeDtypeStruct((groups, length, LANES), F32),
            jax.ShapeDtypeStruct((groups, length, LANES), F32),
        ],
        grid_spec=pltpu.PrefetchScalarGridSpec(
            num_scalar_prefetch=1,
            grid=(groups, tiles),
            in_specs=[
                q_spec,
                pl.BlockSpec((1, length, 2 * LANES), lambda g, t, s: (g, 0, 0)),
                q_spec,
                q_spec,
                pl.BlockSpec((1, 1, 2, rows), lambda g, t, s: (g, t, 0, 0)),
            ],
            out_specs=[q_spec, k_spec, k_spec],
            scratch_shapes=[pltpu.VMEM((LANES, length), BF), pltpu.VMEM((length, rows), F32)],
        ),
        compiler_params=params_of("arbitrary", "arbitrary"),
        cost_estimate=pl.CostEstimate(
            flops=20 * groups * tiles * rows * length * LANES,
            bytes_accessed=query.size * 10 + kv.size * 6,
            transcendentals=groups * tiles * 2 * rows * length,
        ),
        name="prompt_backward",
    )(start, query, kv, out, grad, lse)


def cont_backward_kernel(
    which,
    q_ref,
    kv_ref,
    own_ref,
    o_ref,
    g_ref,
    lse_ref,
    dq_ref,
    dk_ref,
    dv_ref,
    ek_ref,
    ev_ref,
    kt_ref,
    ot_ref,
):
    tile = pl.program_id(1)
    rows = q_ref.shape[1]
    head = tile // (pl.num_programs(1) // 2)

    @pl.when(tile == 0)
    def _():
        kt_ref[...] = kv_ref[0, :, :LANES].astype(F32).T.astype(BF)
        ot_ref[...] = own_ref[0, :, :LANES].astype(F32).T.astype(BF)

    place = pl.ds(pl.multiple_of(head * HEAD_SIZE, HEAD_SIZE), HEAD_SIZE)
    query, grad = q_ref[0], g_ref[0]
    mixed = (grad.astype(F32) * o_ref[0].astype(F32)).T
    delta = jnp.concatenate(
        [
            jnp.sum(mixed[j * HEAD_SIZE : (j + 1) * HEAD_SIZE], axis=0, keepdims=True)
            for j in range(2)
        ],
        axis=1,
    )
    queries = jnp.concatenate([half_of(query, 0), half_of(query, 1)], axis=0)
    grads = jnp.concatenate([half_of(grad, 0), half_of(grad, 1)], axis=0)
    bias = causal_bias(rows, rows, 0)
    lse = lse_ref[0, 0]
    dk, dv, dq = backward_columns(
        doubled(kv_ref[0, :, :LANES], head),
        doubled(kv_ref[0, :, LANES:], head),
        kt_ref[place, :],
        None,
        queries,
        grads,
        lse,
        delta,
        256,
    )
    ek, ev, eq = backward_columns(
        doubled(own_ref[0, :, :LANES], head),
        doubled(own_ref[0, :, LANES:], head),
        ot_ref[place, :],
        jnp.concatenate([bias, bias], axis=1),
        queries,
        grads,
        lse,
        delta,
        rows,
    )
    dq = dq + eq
    dq_ref[0] = jnp.concatenate([dq[:, :rows], dq[:, rows:]], axis=0).T * SCORE_SCALE
    add_into(dk_ref, folded(dk, head) * SCORE_SCALE, tile == 0)
    add_into(dv_ref, folded(dv, head), tile == 0)
    add_into(ek_ref, folded(ek, head) * SCORE_SCALE, tile == 0)
    add_into(ev_ref, folded(ev, head), tile == 0)


def cont_backward(query, kv, own, out, grad, lse, which):
    conts, rows, query_width = query.shape
    length = kv.shape[1]
    tiles = query_width // LANES
    q_spec = pl.BlockSpec((1, rows, LANES), lambda g, t, w: (g, 0, t))
    k_spec = pl.BlockSpec((1, length, LANES), lambda g, t, w: (g, 0, 0))
    e_spec = pl.BlockSpec((1, rows, LANES), lambda g, t, w: (g, 0, 0))
    return pl.pallas_call(
        cont_backward_kernel,
        out_shape=[jax.ShapeDtypeStruct(query.shape, F32)]
        + [jax.ShapeDtypeStruct((conts, length, LANES), F32)] * 2
        + [jax.ShapeDtypeStruct((conts, rows, LANES), F32)] * 2,
        grid_spec=pltpu.PrefetchScalarGridSpec(
            num_scalar_prefetch=1,
            grid=(conts, tiles),
            in_specs=[
                q_spec,
                pl.BlockSpec((1, length, 2 * LANES), lambda g, t, w: (w[g], 0, 0)),
                pl.BlockSpec((1, rows, 2 * LANES), lambda g, t, w: (g, 0, 0)),
                q_spec,
                q_spec,
                pl.BlockSpec((1, 1, 1, 2 * rows), lambda g, t, w: (g, t, 0, 0)),
            ],
            out_specs=[q_spec, k_spec, k_spec, e_spec, e_spec],
            scratch_shapes=[pltpu.VMEM((LANES, length), BF), pltpu.VMEM((LANES, rows), BF)],
        ),
        compiler_params=params_of("arbitrary", "arbitrary"),
        cost_estimate=pl.CostEstimate(
            flops=20 * conts * tiles * rows * (length + rows) * LANES,
            bytes_accessed=query.size * 10 + conts * length * LANES * 12,
            transcendentals=conts * tiles * 2 * rows * (length + rows),
        ),
        name="cont_backward",
    )(which, query, kv, own, out, grad, lse)


def finish_kernel(count, dq_ref, dkv_ref, *refs):
    others = refs[:count]
    q_ref, kv_ref, cosine, sine, out_ref, total_ref = refs[count:]
    query_width = dq_ref.shape[1]
    key_width = dkv_ref.shape[1] // 2
    dkv = dkv_ref[...]
    for other in others:
        dkv = dkv + other[...].astype(F32)
    dq = dq_ref[...]
    total_ref[...] = jnp.sum(dq * q_ref[...].astype(F32), axis=1, keepdims=True) + jnp.sum(
        dkv * kv_ref[...].astype(F32), axis=1, keepdims=True
    )
    back = -sine[...]
    for t in range(query_width // LANES):
        cut = slice(t * LANES, (t + 1) * LANES)
        out_ref[:, cut] = turn(dq[:, cut], cosine[...], back).astype(BF)
    out_ref[:, query_width : query_width + key_width] = turn(
        dkv[:, :key_width], cosine[...], back
    ).astype(BF)
    out_ref[:, query_width + key_width :] = dkv[:, key_width:].astype(BF)


def finish(dq, dkv, others, query, kv, tables):
    rows, query_width = dq.shape
    kv_width = dkv.shape[1]
    block = min(rows, 256)
    row = lambda w: pl.BlockSpec((block, w), lambda i: (i, 0))
    return pl.pallas_call(
        functools.partial(finish_kernel, len(others)),
        out_shape=[
            jax.ShapeDtypeStruct((rows, query_width + kv_width), BF),
            jax.ShapeDtypeStruct((rows, 1), F32),
        ],
        grid=(rows // block,),
        in_specs=[row(query_width)]
        + [row(kv_width)] * (1 + len(others))
        + [row(query_width), row(kv_width), row(LANES), row(LANES)],
        out_specs=[row(query_width + kv_width), row(1)],
        compiler_params=params_of("arbitrary"),
        cost_estimate=pl.CostEstimate(
            flops=20 * dq.size, bytes_accessed=dq.size * 12, transcendentals=0
        ),
        name="finish",
    )(dq, dkv, *others, query, kv, *tables)


def rope_tables(positions):
    lane = jnp.arange(LANES)
    half = HEAD_SIZE // 2
    frequency = ROPE_BASE ** (-(lane % half).astype(F32) * 2.0 / HEAD_SIZE)
    angles = positions.astype(F32)[:, None] * frequency[None, :]
    sign = jnp.where(lane % HEAD_SIZE < half, -1.0, 1.0)
    return jnp.cos(angles), jnp.sin(angles) * sign[None, :]


def second_norm_kernel(count, model_width, order, *refs):
    x, o = refs[:count], refs[count : 2 * count]
    gain, weight, out_ref, hidden_ref, scale_ref = refs[2 * count :]
    width, head_width = x[0].shape[1], o[0].shape[1]
    total = None
    for r, part in enumerate(o):
        term = dot_nn(part[...], weight[r * head_width : (r + 1) * head_width, :])
        total = term if total is None else total + term
    hidden_ref[...] = total
    places = [pl.ds(pl.multiple_of(order[r] * width, width), width) for r in range(count)]
    squares = 0.0
    for place, part in zip(places, x):
        h = hidden_ref[:, place] + part[...].astype(F32)
        hidden_ref[:, place] = h
        squares = squares + jnp.sum(h * h, axis=1, keepdims=True)
    scale = lax.rsqrt(squares / model_width + EPSILON)
    scale_ref[...] = scale
    for r, place in enumerate(places):
        out_ref[:, place] = (hidden_ref[:, place] * scale * gain[r : r + 1, :]).astype(BF)


def spread_kernel(count, order, *refs):
    parts = refs[:count]
    mix, out_ref = refs[count:]
    width = parts[0].shape[1]
    for r, part in enumerate(parts):
        place = pl.ds(pl.multiple_of(order[r] * width, width), width)
        out_ref[:, place] = (part[...].astype(F32) * mix[...]).astype(BF)


def third_norm_kernel(count, model_width, order, *refs):
    cot, n = refs[:count], refs[count : 2 * count]
    gain, scale_ref, mix, hidden_ref, out_ref, factor_ref = refs[2 * count :]
    width = cot[0].shape[1]
    places = [pl.ds(pl.multiple_of(order[r] * width, width), width) for r in range(count)]
    scale = scale_ref[...]
    total = 0.0
    for r, place in enumerate(places):
        total = total + jnp.sum(
            hidden_ref[:, place] * gain[r : r + 1, :] * n[r][...].astype(F32),
            axis=1,
            keepdims=True,
        )
    factor = scale * scale * scale * total / model_width
    factor_ref[...] = factor
    for r, place in enumerate(places):
        value = (
            cot[r][...].astype(F32) * mix[...]
            + scale * gain[r : r + 1, :] * n[r][...].astype(F32)
            - hidden_ref[:, place] * factor
        )
        out_ref[:, place] = value.astype(BF)


def placed_call(kernel, name, order, part_sets, wholes, columns_in, outs, flops=0):
    parts = [p for group in part_sets for p in group]
    rows, width = parts[0].shape
    block = min(rows, 256)
    row = lambda w: pl.BlockSpec((block, w), lambda i, o: (i, 0))
    return pl.pallas_call(
        kernel,
        out_shape=[jax.ShapeDtypeStruct((rows, w), d) for w, d in outs],
        grid_spec=pltpu.PrefetchScalarGridSpec(
            num_scalar_prefetch=1,
            grid=(rows // block,),
            in_specs=[row(p.shape[1]) for p in parts]
            + [pl.BlockSpec(w.shape, lambda i, o: (0, 0)) for w in wholes]
            + [row(c.shape[1]) for c in columns_in],
            out_specs=[row(w) for w, d in outs],
        ),
        compiler_params=params_of("arbitrary"),
        cost_estimate=pl.CostEstimate(
            flops=8 * len(parts) * rows * width + flops,
            bytes_accessed=2 * len(parts) * rows * width,
            transcendentals=rows,
        ),
        name=name,
    )(order, *parts, *wholes, *columns_in)


def second_norm(x, o, gains, weight, order):
    count, width = len(x), x[0].shape[1]
    return placed_call(
        functools.partial(second_norm_kernel, count, count * width),
        "second_norm",
        order,
        [x, o],
        [gains, weight],
        [],
        [(count * width, BF), (count * width, F32), (1, F32)],
        x[0].shape[0] * weight.size * 2,
    )


def spread(parts, mix, order):
    count, width = len(parts), parts[0].shape[1]
    return placed_call(
        functools.partial(spread_kernel, count),
        "spread",
        order,
        [parts],
        [],
        [mix],
        [(count * width, BF)],
    )[0]


def third_norm(hidden, cot, n, gains, scale, mix, order):
    count, width = len(cot), cot[0].shape[1]
    return placed_call(
        functools.partial(third_norm_kernel, count, count * width),
        "third_norm",
        order,
        [cot, n],
        [gains],
        [scale, mix, hidden],
        [(count * width, BF), (1, F32)],
    )


def body(
    prompt_in,
    cont_in,
    prompt_mask,
    cont_mask,
    cont_prompt,
    cont_start,
    gain_attn,
    gain_ffn,
    router,
    w_query,
    key_projection,
    w_value,
    w_out,
    w_gate,
    w_up,
    w_down,
    prompt_cot,
    cont_cot,
):
    groups, prompt_rows, width = prompt_in.shape
    conts = cont_in.shape[0]
    tp_size = lax.axis_size("tp")
    ctx_size = lax.axis_size("ctx")
    model_width = width * tp_size
    me_tp = lax.axis_index("tp")
    me_ctx = lax.axis_index("ctx")
    query_width = w_query.shape[1]
    key_width = key_projection.shape[1]
    kv_width = 2 * key_width
    streams = range(2)
    tokens_in = [prompt_in.reshape(-1, width), cont_in.reshape(-1, width)]
    cots = [prompt_cot.reshape(-1, width), cont_cot.reshape(-1, width)]
    masks = [prompt_mask.reshape(-1, 1).astype(F32), cont_mask.reshape(-1, 1).astype(F32)]
    prompt_place = me_ctx * prompt_rows + jnp.arange(prompt_rows, dtype=jnp.int32)
    cont_place = (
        cont_start[:, None] + jnp.arange(CONTINUATION_LEN, dtype=jnp.int32)[None, :]
    ).reshape(-1)
    tables = [rope_tables(jnp.tile(prompt_place, groups)), rope_tables(cont_place)]
    local_prompt = jnp.clip(cont_prompt - lax.axis_index("fsdp") * groups, 0, groups - 1)
    start = (me_ctx * prompt_rows).astype(jnp.int32)[None]
    order = jnp.stack([me_tp ^ step for step in range(tp_size)]).astype(jnp.int32)

    full_qkv, qkv_far = gather_weight(
        jnp.concatenate([w_query, key_projection, w_value], axis=1), 0
    )
    params = [p.astype(F32) for p in pieces_of(jnp.stack([gain_attn, gain_ffn, router]))]
    gains_attn = jnp.stack([p[0] for p in params])
    gains_ffn = jnp.stack([p[1] for p in params])
    routers = jnp.stack([p[2] for p in params])
    full_out, sent_out = gather_out(w_out)
    x_prompt, sent_prompt = gather_tp(tie(tokens_in[0], sent_out))
    x_cont, sent_cont = gather_tp(tie(tokens_in[1], sent_prompt))
    x_parts = [x_prompt, x_cont]
    full_gate, gate_far = gather_weight(w_gate, 0, qkv_far)
    full_up, up_far = gather_weight(w_up, 0, gate_far)
    full_down = gather_weight_offload(w_down, 1, sent_prompt)

    def enter(i):
        return entry(
            x_parts[i], gains_attn, routers, full_qkv, masks[i], tables[i], order, query_width
        )

    xn1, query, kv, scale_attn, gate_router, mixing = zip(enter(0), enter(1))
    own_kv = kv[0].reshape(groups, prompt_rows, kv_width)
    prompt_kv = jnp.zeros((groups, prompt_rows * ctx_size, kv_width), BF)
    for step, part in enumerate(pieces_of(own_kv, "ctx")):
        prompt_kv = lax.dynamic_update_slice(prompt_kv, part, (0, (me_ctx ^ step) * prompt_rows, 0))
    queries = [
        query[0].reshape(groups, prompt_rows, query_width),
        query[1].reshape(conts, CONTINUATION_LEN, query_width),
    ]
    cont_kv = kv[1].reshape(conts, CONTINUATION_LEN, kv_width)
    prompt_o, prompt_lse = prompt_forward(queries[0], prompt_kv, start)
    cont_o, cont_lse = cont_forward(queries[1], prompt_kv, cont_kv, local_prompt)
    attended = [prompt_o.reshape(-1, query_width), cont_o.reshape(-1, query_width)]
    o_prompt, sent_prompt = gather_tp(attended[0])
    o_cont, sent_cont = gather_tp(tie(attended[1], sent_prompt))
    cot_cont, sent_cont = gather_tp(tie(cots[1], sent_cont))
    cot_prompt, sent_prompt = gather_tp(tie(cots[0], sent_cont))
    o_parts, cot_parts = [o_prompt, o_cont], [cot_prompt, cot_cont]

    xn2, hidden, scale_ffn = zip(
        *[second_norm(x_parts[i], o_parts[i], gains_ffn, full_out, order) for i in streams]
    )

    inner, gate_grad, up_grad = [None, None], [None, None], [None, None]
    ffn_grad, blocks = [None, None], [None, None]
    for i in (1, 0):
        g = product(xn2[i], full_gate)
        u = product(xn2[i], full_up)
        s = jax.nn.sigmoid(g)
        inner[i] = (g * s * u).astype(BF)
        ffn_grad[i] = spread(cot_parts[i], mixing[i], order)
        dz = product_nt(ffn_grad[i], full_down)
        gate_grad[i] = (dz * u * s * (1.0 + g * (1.0 - s))).astype(BF)
        up_grad[i] = (dz * g * s).astype(BF)
        blocks[i] = blocks_of(
            lambda b, i=i: product_nt(gate_grad[i], rows_of(full_gate, b, width))
            + product_nt(up_grad[i], rows_of(full_up, b, width))
        )

    both = lambda pair: jnp.concatenate(pair, axis=0)
    normed_grad = [None, exchange_sum(blocks[1])]
    blocks[0], normed_grad[1] = lax.optimization_barrier((blocks[0], normed_grad[1]))
    normed_grad[0] = exchange_sum(blocks[0])
    n_cont, sent_cont = gather_tp(normed_grad[1].astype(BF))
    xn2_all, ffn_grad_all, inner_all, gate_all, up_all = tie(
        (both(xn2), both(ffn_grad), both(inner), both(gate_grad), both(up_grad)), blocks[0]
    )
    started = [
        grad_start(xn2_all, gate_all, 0),
        grad_start(xn2_all, up_all, 0),
        grad_start(inner_all, ffn_grad_all, 1),
    ]
    late = tie(normed_grad[0].astype(BF), (sent_cont, [s[2] for s in started]))
    n_prompt, sent_prompt = gather_tp(late)
    n_parts = [n_prompt, n_cont]
    inner_late = tie(inner, normed_grad[0])
    ffn_blocks = [
        blocks_of(lambda b, t=t: product(t, columns(full_down, b, width))) for t in inner_late
    ]

    def third(i):
        return third_norm(
            hidden[i], cot_parts[i], n_parts[i], gains_ffn, scale_ffn[i], mixing[i], order
        )

    middle = [grad_middle(*started[i], axis) for i, axis in enumerate((0, 0, 1))]
    dab_cont, factor_cont = third(1)
    dab_cont = tie(dab_cont, started[0][0])
    do_cont = product_nt(dab_cont, full_out[:query_width]).astype(BF)
    dq_cont, dk_cont, dv_cont, dk_own, dv_own = cont_backward(
        queries[1],
        prompt_kv,
        cont_kv,
        cont_o,
        do_cont.reshape(queries[1].shape),
        cont_lse,
        local_prompt,
    )
    dab_prompt, factor_prompt = third(0)
    dab_prompt = tie(dab_prompt, (middle[0], started[1][0]))
    do_prompt = product_nt(dab_prompt, full_out[:query_width]).astype(BF)
    dab, factor = [dab_prompt, dab_cont], [factor_prompt, factor_cont]
    ffn_blocks, do_prompt = lax.optimization_barrier((ffn_blocks, do_prompt))
    branch_ffn = [None, exchange_sum(ffn_blocks[1])]
    ffn_blocks[0] = tie(ffn_blocks[0], branch_ffn[1])
    branch_ffn[0] = exchange_sum(ffn_blocks[0])
    dq_prompt, dk_prompt, dv_prompt = prompt_backward(
        queries[0], prompt_kv, prompt_o, do_prompt.reshape(queries[0].shape), prompt_lse, start
    )
    dq_prompt = tie(dq_prompt, branch_ffn[1])
    started_out = grad_start(both(attended), both(dab), 1)
    chosen = (local_prompt[:, None] == jnp.arange(groups, dtype=jnp.int32)[None, :]).astype(F32)

    def kv_block(step):
        place = (me_ctx ^ step) * prompt_rows

        def piece(whole):
            return lax.dynamic_slice(
                whole, (0, place, 0), (whole.shape[0], prompt_rows, whole.shape[2])
            )

        def total(prompts, extra):
            extra = piece(extra)
            sums = [
                sum(chosen[c, g] * extra[c] for c in range(conts)) for g in range(groups)
            ]
            return piece(prompts) + jnp.stack(sums)

        return jnp.concatenate(
            [total(dk_prompt, dk_cont), total(dv_prompt, dv_cont)], axis=2
        ).reshape(-1, kv_width)

    sent = [swap(kv_block(step).astype(BF), "ctx", step) for step in range(1, ctx_size)]
    dkv_own = jnp.concatenate([dk_own, dv_own], axis=2).reshape(-1, kv_width)
    finished_cont = finish(
        dq_cont.reshape(-1, query_width), dkv_own, [], query[1], kv[1], tables[1]
    )
    finished = [
        finish(dq_prompt.reshape(-1, query_width), kv_block(0), sent, query[0], kv[0], tables[0]),
        finished_cont,
    ]
    dqkv = [f[0] for f in finished]
    attn_blocks = [
        blocks_of(lambda b, t=t: product_nt(t, rows_of(full_qkv, b, width))) for t in dqkv
    ]
    attn_blocks = tie(attn_blocks, (middle[1], branch_ffn[0], started[2][0]))
    normed_attn_grad = [None, exchange_sum(attn_blocks[1])]
    attn_blocks[0] = tie(attn_blocks[0], normed_attn_grad[1])
    normed_attn_grad[0] = exchange_sum(attn_blocks[0])
    sizes = [t.shape[0] for t in dqkv]
    joined = lambda pair: jnp.concatenate([p.reshape(-1, LANES) for p in pair], axis=0)
    parted = lambda t: [
        p.reshape(-1, 1) for p in jnp.split(t, [sizes[0] // LANES], axis=0)
    ]
    total_attn = parted(all_sum(joined([f[1] for f in finished])))
    qkv_left, qkv_right = tie((both(xn1), both(dqkv)), attn_blocks)
    started_qkv = grad_start(qkv_left, qkv_right, 0)
    middle.append(grad_middle(*started_out, 1))
    middle.append(grad_middle(*started_qkv, 0))
    grad_gate, grad_up, grad_down, grad_out, grad_qkv = [
        grad_end(middle[i], axis) for i, axis in enumerate((0, 0, 1, 1, 0))
    ]

    gain_attn_sum, gain_ffn_sum, router_sum = 0.0, 0.0, 0.0
    outs, token_grads = [], []
    hidden_own = [columns(h, me_tp, width) for h in hidden]
    branch = [
        hidden_own[i] - tokens_in[i].astype(F32) + branch_ffn[i] for i in streams
    ]
    sums = parted(
        all_sum(
            joined(
                [
                    jnp.sum(cots[i].astype(F32) * mixing[i] * branch[i], axis=1, keepdims=True)
                    for i in streams
                ]
            )
        )
    )
    for i in streams:
        x = tokens_in[i].astype(F32)
        dy = cots[i].astype(F32)
        outs.append((x + mixing[i] * branch[i]).astype(BF))
        dl = (1.0 - gate_router[i]) * sums[i]
        router_sum = router_sum + jnp.sum(x * dl, axis=0)
        gain_ffn_sum = gain_ffn_sum + jnp.sum(
            hidden_own[i] * scale_ffn[i] * normed_grad[i], axis=0
        )
        back_ffn = scale_ffn[i] * gains_ffn[0:1] * normed_grad[i] - hidden_own[i] * factor[i]
        scale = scale_attn[i]
        n = normed_attn_grad[i]
        gain_attn_sum = gain_attn_sum + jnp.sum(x * scale * n, axis=0)
        n1 = scale * gains_attn[0:1] * n - x * (scale * scale * total_attn[i] / model_width)
        token_grads.append(dy + dl * routers[0:1] + back_ffn + n1)
    early = group_sum(jnp.stack([gain_ffn_sum, router_sum]))
    small = [group_sum(gain_attn_sum), early[0], early[1]]
    return (
        outs[0].reshape(prompt_in.shape),
        outs[1].reshape(cont_in.shape),
        token_grads[0].reshape(prompt_in.shape),
        token_grads[1].reshape(cont_in.shape),
        small[0],
        small[1],
        small[2],
        grad_qkv[:, :query_width],
        grad_qkv[:, query_width : query_width + key_width],
        grad_qkv[:, query_width + key_width :],
        grad_out,
        grad_gate,
        grad_up,
        grad_down,
    )


def solution(mesh):
    placed = (
        P("fsdp", "ctx", "tp"),
        P(("fsdp", "ctx"), None, "tp"),
        P("fsdp", "ctx"),
        P(("fsdp", "ctx"), None),
        P(("fsdp", "ctx")),
        P(("fsdp", "ctx")),
        P("tp"),
        P("tp"),
        P("tp"),
        P("fsdp", "tp"),
        P("fsdp", "tp"),
        P("fsdp", "tp"),
        P("tp", "fsdp"),
        P("fsdp", "tp"),
        P("fsdp", "tp"),
        P("tp", "fsdp"),
        P("fsdp", "ctx", "tp"),
        P(("fsdp", "ctx"), None, "tp"),
    )
    return jax.shard_map(
        body,
        mesh=mesh,
        in_specs=placed,
        out_specs=(
            P("fsdp", "ctx", "tp"),
            P(("fsdp", "ctx"), None, "tp"),
            P("fsdp", "ctx", "tp"),
            P(("fsdp", "ctx"), None, "tp"),
            P("tp"),
            P("tp"),
            P("tp"),
            P("fsdp", "tp"),
            P("fsdp", "tp"),
            P("fsdp", "tp"),
            P("tp", "fsdp"),
            P("fsdp", "tp"),
            P("fsdp", "tp"),
            P("tp", "fsdp"),
        ),
        check_vma=False,
    )
```

```python
import functools

import jax
import jax.numpy as jnp
from jax import lax
from jax.experimental import pallas as pl
from jax.experimental.pallas import tpu as pltpu
from jax.sharding import PartitionSpec as P

HEAD_SIZE = 64
CONTINUATION_LEN = 128
EPSILON = 1e-05
ROPE_BASE = 500000.0
BF = jnp.bfloat16
F32 = jnp.float32
EVERY = ("fsdp", "ctx")


def product(left, right):
    return jnp.dot(left, right, preferred_element_type=F32)


def product_nt(left, right):
    return lax.dot_general(left, right, (((1,), (1,)), ((), ())), preferred_element_type=F32)


def product_tn(left, right):
    return lax.dot_general(left, right, (((0,), (0,)), ((), ())), preferred_element_type=F32)


def swap(value, axis, step):
    count = lax.axis_size(axis)
    return lax.ppermute(value, axis, [(i, i ^ step) for i in range(count)])


def pieces_of(value, axis="tp"):
    return [value] + [swap(value, axis, step) for step in range(1, lax.axis_size(axis))]


def tie(values, deps):
    return lax.optimization_barrier((values, deps))[0]


def inner_pair():
    me = lax.axis_index("tp")
    return (me == 1) | (me == 2)


def gather_tp(value, before=None):
    if lax.axis_size("tp") != 4:
        parts = pieces_of(value)
        return parts, parts[1:]
    second = swap(value, "tp", 2)
    first = swap(value, "tp", 1)
    middle = lax.ppermute(value, "tp", [(1, 2), (2, 1)])
    ready = tie(second, first if before is None else (first, before))
    passed = lax.ppermute(ready, "tp", [(2, 3), (1, 0)])
    third = jnp.where(inner_pair(), middle, passed)
    return [value, first, second, third], [first, second, middle, passed]


def all_sum(value, axis="tp"):
    parts = pieces_of(value, axis)
    total = parts[0]
    for part in parts[1:]:
        total = total + part
    return total


def group_sum(value):
    if not paired():
        return lax.psum(value, EVERY)
    for axis, step in (("ctx", 1), ("ctx", 2), ("fsdp", 1)):
        value = value + swap(value, axis, step)
    return value


def blocks_of(make_block):
    me = lax.axis_index("tp")
    blocks = [make_block(me ^ step) for step in range(lax.axis_size("tp"))]
    if len(blocks) != 4:
        return [blocks[0]] + [block.astype(BF) for block in blocks[1:]]
    return [blocks[0], blocks[1].astype(BF), blocks[2], blocks[3].astype(BF)]


def exchange_direct(blocks):
    sent = [swap(block.astype(BF), "tp", step) for step, block in enumerate(blocks) if step > 0]
    total = blocks[0]
    for part in sent:
        total = total + part.astype(F32)
    return total, sent


def exchange_sum(blocks, after=()):
    if len(blocks) != 4:
        sent = [swap(block, "tp", step) for step, block in enumerate(blocks) if step > 0]
        early, phase = sent[0], sent
    else:
        passed = lax.ppermute(blocks[3], "tp", [(3, 2), (0, 1)])
        middle = lax.ppermute(blocks[3], "tp", [(1, 2), (2, 1)])
        first = swap(blocks[1], "tp", 1)
        phase = [passed, middle, first]
        passed, middle, first = tie(phase, after)
        early = (blocks[2] + passed.astype(F32)).astype(BF)
        sent = [middle, first, swap(early, "tp", 2)]
    total = blocks[0]
    for part in sent:
        total = total + part.astype(F32)
    return total, early, phase


def columns(matrix, block, width):
    return lax.dynamic_slice(matrix, (0, block * width), (matrix.shape[0], width))


def rows_of(matrix, block, width):
    return lax.dynamic_slice(matrix, (block * width, 0), (width, matrix.shape[1]))


def cut_of(matrix, axis, block, width):
    return rows_of(matrix, block, width) if axis == 0 else columns(matrix, block, width)


def paired():
    return lax.axis_size("fsdp") == 2 and lax.axis_size("ctx") == 4


def gather_weight(weight, axis, after=None):
    me = lax.axis_index("ctx")
    size = weight.shape[axis] // lax.axis_size("ctx")
    if not paired():
        quarter = cut_of(weight, axis, me, size)
        return [quarter] * 2, lambda after: lax.all_gather(quarter, EVERY, axis=axis, tiled=True)
    if after is not None:
        weight = tie(weight, after)
    mine = lax.axis_index("fsdp")
    far = swap(cut_of(weight, axis, me, size), "fsdp", 1)
    across = swap(far, "ctx", 2)
    found = [(0, far), (2, across), (1, swap(far, "ctx", 1)), (3, swap(across, "ctx", 1))]
    shape = list(weight.shape)
    shape[axis] *= 2
    at = lambda start: (start, 0) if axis == 0 else (0, start)

    def whole(after):
        own = weight if after is None else tie(weight, after)
        result = lax.dynamic_update_slice(
            jnp.zeros(shape, weight.dtype), own, at(mine * size * 4)
        )
        for step, part in found:
            result = lax.dynamic_update_slice(
                result, part, at(((1 - mine) * 4 + (me ^ step)) * size)
            )
        return result

    return [far, across], whole


def gather_out(weight, after):
    if not paired():
        pieces, done = gather_tp(lax.all_gather(weight, "fsdp", axis=1, tiled=True))
        return done, pieces, lambda after: jnp.concatenate(pieces, axis=0)
    me = lax.axis_index("ctx")
    mine = lax.axis_index("fsdp")
    size = weight.shape[1] // lax.axis_size("ctx")
    pieces, done = gather_tp(tie(columns(weight, me, size), after))
    own = jnp.concatenate(pieces, axis=0)
    far = swap(own, "fsdp", 1)
    across = swap(own, "ctx", 2)
    far_across = swap(across, "fsdp", 1)
    found = [(mine, 0, own), (1 - mine, 0, far), (mine, 2, across), (1 - mine, 2, far_across)]
    found += [(f, step ^ 1, swap(part, "ctx", 1)) for f, step, part in found]

    def whole(after):
        result = jnp.zeros((own.shape[0], size * 8), weight.dtype)
        for f, step, part in found:
            result = lax.dynamic_update_slice(result, part, (0, (f * 4 + (me ^ step)) * size))
        return result

    return done, [far, across, far_across], whole


def scatter_grad(part, axis):
    return lax.psum_scatter(part, EVERY, scatter_dimension=axis, tiled=True)


def spread_grad(piece, across, axis):
    if not paired():
        return lax.all_gather(piece, "ctx", axis=axis, tiled=True).astype(F32)
    low_side = lax.axis_index("ctx") // 2 == 0
    low_core = lax.axis_index("ctx") % 2 == 0
    pair = [jnp.where(low_side, piece, across), jnp.where(low_side, across, piece)]
    parts = []
    for mine, theirs in zip(pair, [swap(p, "ctx", 1) for p in pair]):
        parts += [jnp.where(low_core, mine, theirs), jnp.where(low_core, theirs, mine)]
    return jnp.concatenate(parts, axis=axis).astype(F32)


def grad_start(left, right, axis):
    if not paired():
        whole = product_tn(left, right).astype(BF)
        return whole, whole, whole
    mine = lax.axis_index("fsdp")
    core = lax.axis_index("ctx") % 2
    split, other = (left, right) if axis == 0 else (right, left)
    half = lambda m, i: columns(m, i, m.shape[1] // 2)
    split_far, split_own = half(split, 1 - mine), half(split, mine)
    other_far, other_own = half(other, 1 - core), half(other, core)
    dot = lambda s, t: product_tn(s, t) if axis == 0 else product_tn(t, s)
    first = swap(dot(split_far, other_far).astype(BF), "ctx", 1)
    far = (dot(split_far, other_own) + first.astype(F32)).astype(BF)
    split_own = tie(split_own, far)
    second = swap(dot(split_own, other_far).astype(BF), "ctx", 1)
    kept = dot(split_own, other_own) + second.astype(F32)
    return swap(far, "fsdp", 1), kept, far


def grad_middle(arrived, kept, far, axis):
    if not paired():
        return lax.psum_scatter(kept, EVERY, scatter_dimension=axis, tiled=True)
    side = lax.axis_index("ctx") // 2
    size = kept.shape[axis] // 2
    half = lambda i: cut_of(kept, axis, i, size) + cut_of(arrived, axis, i, size).astype(F32)
    sent = swap(half(1 - side).astype(BF), "ctx", 2)
    return (half(side) + sent.astype(F32)).astype(BF)


def grad_end(piece, axis):
    if not paired():
        return lax.all_gather(piece, "ctx", axis=axis, tiled=True).astype(F32)
    side = lax.axis_index("ctx") // 2
    core = lax.axis_index("ctx") % 2
    across = swap(piece, "ctx", 2)
    own = in_order(piece, across, side, axis)
    return in_order(own, swap(own, "ctx", 1), core, 1 - axis).astype(F32)


def in_order(mine, theirs, index, axis):
    low = index == 0
    return jnp.concatenate(
        [jnp.where(low, mine, theirs), jnp.where(low, theirs, mine)], axis=axis
    )


LOG2E = 1.4426950408889634
SCORE_SCALE = 0.125
LANES = 128


def lane_index(shape):
    return lax.broadcasted_iota(jnp.int32, shape, len(shape) - 1)


def turn(tile, cosine, sine):
    low = lane_index(tile.shape) % HEAD_SIZE < HEAD_SIZE // 2
    other = jnp.where(
        low,
        pltpu.roll(tile, LANES - HEAD_SIZE // 2, 1),
        pltpu.roll(tile, HEAD_SIZE // 2, 1),
    )
    return tile * cosine + other * sine


def doubled(tile, head):
    wide = tile.astype(F32)
    low = lane_index(tile.shape) < HEAD_SIZE
    other = pltpu.roll(wide, HEAD_SIZE, 1)
    return jnp.where(low == (head == 0), wide, other).astype(tile.dtype)


def half_of(tile, j):
    low = lane_index(tile.shape) < HEAD_SIZE
    keep = low if j == 0 else jnp.logical_not(low)
    return jnp.where(keep, tile, jnp.zeros_like(tile))


def dot_nt(left, right):
    return lax.dot_general(left, right, (((1,), (1,)), ((), ())), preferred_element_type=F32)


def dot_nn(left, right):
    return lax.dot_general(left, right, (((1,), (0,)), ((), ())), preferred_element_type=F32)


def params_of(*semantics, limit=56 << 20):
    return pltpu.CompilerParams(dimension_semantics=semantics, vmem_limit_bytes=limit)


def entry_kernel(count, model_width, query_width, order, *refs):
    parts = refs[:count]
    gain, router, weight, mask, cosine, sine = refs[count : count + 6]
    xn_ref, query_ref, kv_ref, scale_ref, gate_ref, mix_ref = refs[count + 6 :]
    width = parts[0].shape[1]
    wide = [p[...].astype(F32) for p in parts]
    squares = sum(jnp.sum(w * w, axis=1, keepdims=True) for w in wide)
    logits = sum(
        jnp.sum(w * router[r : r + 1, :], axis=1, keepdims=True) for r, w in enumerate(wide)
    )
    scale = lax.rsqrt(squares / model_width + EPSILON)
    gate = jax.nn.sigmoid(logits)
    scale_ref[...] = scale
    gate_ref[...] = gate
    mix_ref[...] = mask[...] * gate
    total = None
    for r, w in enumerate(wide):
        normed = (w * scale * gain[r : r + 1, :]).astype(BF)
        place = pl.ds(pl.multiple_of(order[r] * width, width), width)
        xn_ref[:, place] = normed
        term = dot_nn(normed, weight[place, :])
        total = term if total is None else total + term
    for t in range(query_width // LANES):
        cut = slice(t * LANES, (t + 1) * LANES)
        query_ref[:, cut] = turn(total[:, cut], cosine[...], sine[...]).astype(BF)
    key_width = kv_ref.shape[1] // 2
    key = total[:, query_width : query_width + key_width]
    kv_ref[:, :key_width] = turn(key, cosine[...], sine[...]).astype(BF)
    kv_ref[:, key_width:] = total[:, query_width + key_width :].astype(BF)


def entry(parts, gains, routers, weight, mask, tables, order, query_width):
    rows, width = parts[0].shape
    count = len(parts)
    block = min(rows, 256)
    total_width = weight.shape[1]
    kv_width = total_width - query_width
    whole = lambda a: pl.BlockSpec(a.shape, lambda i, o: (0, 0))
    row = lambda w: pl.BlockSpec((block, w), lambda i, o: (i, 0))
    outs = [(width * count, BF), (query_width, BF), (kv_width, BF), (1, F32), (1, F32), (1, F32)]
    return pl.pallas_call(
        functools.partial(entry_kernel, count, width * count, query_width),
        out_shape=[jax.ShapeDtypeStruct((rows, w), d) for w, d in outs],
        grid_spec=pltpu.PrefetchScalarGridSpec(
            num_scalar_prefetch=1,
            grid=(rows // block,),
            in_specs=[row(width)] * count
            + [whole(gains), whole(routers), whole(weight), row(1), row(LANES), row(LANES)],
            out_specs=[row(w) for w, d in outs],
        ),
        compiler_params=params_of("arbitrary"),
        cost_estimate=pl.CostEstimate(
            flops=2 * rows * width * count * total_width,
            bytes_accessed=rows * width * count * 4 + weight.size * 2,
            transcendentals=rows,
        ),
        name="entry",
    )(order, *parts, gains, routers, weight, mask, *tables)


def softmax_columns(keys, biases, queries, scores):
    top = None
    for i, (key, bias) in enumerate(zip(keys, biases)):
        s = dot_nt(key, queries) * (SCORE_SCALE * LOG2E)
        if bias is not None:
            s = s + bias
        scores[i][...] = s
        part = jnp.max(s, axis=0, keepdims=True)
        top = part if top is None else jnp.maximum(top, part)
    total = 0.0
    for ref in scores:
        e = jnp.exp2(ref[...] - top)
        ref[...] = e
        total = total + jnp.sum(e, axis=0, keepdims=True)
    share = 1.0 / total
    return [(ref[...] * share).astype(BF) for ref in scores], top + jnp.log2(total)


def causal_bias(keys, rows, start):
    key = lax.broadcasted_iota(jnp.int32, (keys, rows), 0)
    row = lax.broadcasted_iota(jnp.int32, (keys, rows), 1)
    return jnp.where(key <= row + start, 0.0, -1e30)


def prompt_forward_kernel(start, q_ref, kv_ref, o_ref, lse_ref, vt_ref, bias_ref, s_ref):
    tile = pl.program_id(1)
    rows = q_ref.shape[1]
    head = tile // (pl.num_programs(1) // 2)

    @pl.when((pl.program_id(0) == 0) & (tile == 0))
    def _():
        bias_ref[...] = causal_bias(bias_ref.shape[0], rows, start[0])

    @pl.when(tile == 0)
    def _():
        vt_ref[...] = kv_ref[0, :, LANES:].astype(F32).T.astype(BF)

    key = doubled(kv_ref[0, :, :LANES], head)
    value_t = vt_ref[pl.ds(pl.multiple_of(head * HEAD_SIZE, HEAD_SIZE), HEAD_SIZE), :]
    query = q_ref[0]
    outs = []
    for j in range(2):
        probs, lse = softmax_columns([key], [bias_ref[...]], half_of(query, j), [s_ref])
        lse_ref[0, 0, j : j + 1, :] = lse
        outs.append(dot_nn(value_t, probs[0]))
    o_ref[0] = jnp.concatenate(outs, axis=0).T.astype(BF)


def prompt_forward(query, kv, start):
    groups, rows, query_width = query.shape
    length = kv.shape[1]
    tiles = query_width // LANES
    return pl.pallas_call(
        prompt_forward_kernel,
        out_shape=[
            jax.ShapeDtypeStruct(query.shape, BF),
            jax.ShapeDtypeStruct((groups, tiles, 2, rows), F32),
        ],
        grid_spec=pltpu.PrefetchScalarGridSpec(
            num_scalar_prefetch=1,
            grid=(groups, tiles),
            in_specs=[
                pl.BlockSpec((1, rows, LANES), lambda g, t, s: (g, 0, t)),
                pl.BlockSpec((1, length, 2 * LANES), lambda g, t, s: (g, 0, 0)),
            ],
            out_specs=[
                pl.BlockSpec((1, rows, LANES), lambda g, t, s: (g, 0, t)),
                pl.BlockSpec((1, 1, 2, rows), lambda g, t, s: (g, t, 0, 0)),
            ],
            scratch_shapes=[
                pltpu.VMEM((LANES, length), BF),
                pltpu.VMEM((length, rows), F32),
                pltpu.VMEM((length, rows), F32),
            ],
        ),
        compiler_params=params_of("arbitrary", "arbitrary"),
        cost_estimate=pl.CostEstimate(
            flops=8 * groups * tiles * rows * length * LANES,
            bytes_accessed=query.size * 4 + kv.size * 2,
            transcendentals=groups * tiles * 2 * rows * length,
        ),
        name="prompt_forward",
    )(start, query, kv)


def cont_forward_kernel(which, q_ref, kv_ref, own_ref, o_ref, lse_ref, vt_ref, wt_ref, s_ref, t_ref):
    tile = pl.program_id(1)
    rows = q_ref.shape[1]
    head = tile // (pl.num_programs(1) // 2)

    @pl.when(tile == 0)
    def _():
        vt_ref[...] = kv_ref[0, :, LANES:].astype(F32).T.astype(BF)
        wt_ref[...] = own_ref[0, :, LANES:].astype(F32).T.astype(BF)

    place = pl.ds(pl.multiple_of(head * HEAD_SIZE, HEAD_SIZE), HEAD_SIZE)
    keys = [doubled(kv_ref[0, :, :LANES], head), doubled(own_ref[0, :, :LANES], head)]
    query = q_ref[0]
    both = jnp.concatenate([half_of(query, 0), half_of(query, 1)], axis=0)
    bias = causal_bias(rows, rows, 0)
    probs, lse = softmax_columns(
        keys, [None, jnp.concatenate([bias, bias], axis=1)], both, [s_ref, t_ref]
    )
    out = dot_nn(vt_ref[place, :], probs[0]) + dot_nn(wt_ref[place, :], probs[1])
    lse_ref[0, 0] = lse
    o_ref[0] = jnp.concatenate([out[:, :rows], out[:, rows:]], axis=0).T.astype(BF)


def cont_forward(query, kv, own, which):
    conts, rows, query_width = query.shape
    length = kv.shape[1]
    tiles = query_width // LANES
    return pl.pallas_call(
        cont_forward_kernel,
        out_shape=[
            jax.ShapeDtypeStruct(query.shape, BF),
            jax.ShapeDtypeStruct((conts, tiles, 1, 2 * rows), F32),
        ],
        grid_spec=pltpu.PrefetchScalarGridSpec(
            num_scalar_prefetch=1,
            grid=(conts, tiles),
            in_specs=[
                pl.BlockSpec((1, rows, LANES), lambda g, t, w: (g, 0, t)),
                pl.BlockSpec((1, length, 2 * LANES), lambda g, t, w: (w[g], 0, 0)),
                pl.BlockSpec((1, rows, 2 * LANES), lambda g, t, w: (g, 0, 0)),
            ],
            out_specs=[
                pl.BlockSpec((1, rows, LANES), lambda g, t, w: (g, 0, t)),
                pl.BlockSpec((1, 1, 1, 2 * rows), lambda g, t, w: (g, t, 0, 0)),
            ],
            scratch_shapes=[
                pltpu.VMEM((LANES, length), BF),
                pltpu.VMEM((LANES, rows), BF),
                pltpu.VMEM((length, 2 * rows), F32),
                pltpu.VMEM((rows, 2 * rows), F32),
            ],
        ),
        compiler_params=params_of("arbitrary", "arbitrary"),
        cost_estimate=pl.CostEstimate(
            flops=8 * conts * tiles * rows * (length + rows) * LANES,
            bytes_accessed=query.size * 4 + conts * length * LANES * 4,
            transcendentals=conts * tiles * 2 * rows * (length + rows),
        ),
        name="cont_forward",
    )(which, query, kv, own)


def backward_columns(key, value, key_t, bias, query, grad, lse, delta, chunk):
    dks, dvs, dq = [], [], None
    for c in range(key.shape[0] // chunk):
        cut = slice(c * chunk, (c + 1) * chunk)
        s = dot_nt(key[cut], query) * (SCORE_SCALE * LOG2E)
        if bias is not None:
            s = s + bias[cut]
        p = jnp.exp2(s - lse)
        dp = dot_nt(value[cut], grad)
        ds = (p * (dp - delta)).astype(BF)
        dvs.append(dot_nn(p.astype(BF), grad))
        dks.append(dot_nn(ds, query))
        term = dot_nn(key_t[:, cut], ds)
        dq = term if dq is None else dq + term
    return dks, dvs, dq


def folded(parts, head):
    whole = jnp.concatenate(parts, axis=0)
    low = lane_index(whole.shape) < HEAD_SIZE
    return jnp.where(low == (head == 0), whole + pltpu.roll(whole, HEAD_SIZE, 1), 0.0)


def add_into(ref, value, first):
    @pl.when(first)
    def _():
        ref[0] = value

    @pl.when(jnp.logical_not(first))
    def _():
        ref[0] = ref[0] + value


def prompt_backward_kernel(
    start, q_ref, kv_ref, o_ref, g_ref, lse_ref, dq_ref, dk_ref, dv_ref, kt_ref, bias_ref
):
    tile = pl.program_id(1)
    rows = q_ref.shape[1]
    head = tile // (pl.num_programs(1) // 2)

    @pl.when((pl.program_id(0) == 0) & (tile == 0))
    def _():
        bias_ref[...] = causal_bias(bias_ref.shape[0], rows, start[0])

    @pl.when(tile == 0)
    def _():
        kt_ref[...] = kv_ref[0, :, :LANES].astype(F32).T.astype(BF)

    key = doubled(kv_ref[0, :, :LANES], head)
    value = doubled(kv_ref[0, :, LANES:], head)
    key_t = kt_ref[pl.ds(pl.multiple_of(head * HEAD_SIZE, HEAD_SIZE), HEAD_SIZE), :]
    query, grad = q_ref[0], g_ref[0]
    mixed = (grad.astype(F32) * o_ref[0].astype(F32)).T
    dks, dvs, dqs = None, None, []
    for j in range(2):
        delta = jnp.sum(mixed[j * HEAD_SIZE : (j + 1) * HEAD_SIZE], axis=0, keepdims=True)
        dk, dv, dq = backward_columns(
            key,
            value,
            key_t,
            bias_ref,
            half_of(query, j),
            half_of(grad, j),
            lse_ref[0, 0, j : j + 1, :],
            delta,
            256,
        )
        dks = dk if dks is None else [a + b for a, b in zip(dks, dk)]
        dvs = dv if dvs is None else [a + b for a, b in zip(dvs, dv)]
        dqs.append(dq)
    dq_ref[0] = jnp.concatenate(dqs, axis=0).T * SCORE_SCALE
    add_into(dk_ref, folded(dks, head) * SCORE_SCALE, tile == 0)
    add_into(dv_ref, folded(dvs, head), tile == 0)


def prompt_backward(query, kv, out, grad, lse, start):
    groups, rows, query_width = query.shape
    length = kv.shape[1]
    tiles = query_width // LANES
    q_spec = pl.BlockSpec((1, rows, LANES), lambda g, t, s: (g, 0, t))
    k_spec = pl.BlockSpec((1, length, LANES), lambda g, t, s: (g, 0, 0))
    return pl.pallas_call(
        prompt_backward_kernel,
        out_shape=[
            jax.ShapeDtypeStruct(query.shape, F32),
            jax.ShapeDtypeStruct((groups, length, LANES), F32),
            jax.ShapeDtypeStruct((groups, length, LANES), F32),
        ],
        grid_spec=pltpu.PrefetchScalarGridSpec(
            num_scalar_prefetch=1,
            grid=(groups, tiles),
            in_specs=[
                q_spec,
                pl.BlockSpec((1, length, 2 * LANES), lambda g, t, s: (g, 0, 0)),
                q_spec,
                q_spec,
                pl.BlockSpec((1, 1, 2, rows), lambda g, t, s: (g, t, 0, 0)),
            ],
            out_specs=[q_spec, k_spec, k_spec],
            scratch_shapes=[pltpu.VMEM((LANES, length), BF), pltpu.VMEM((length, rows), F32)],
        ),
        compiler_params=params_of("arbitrary", "arbitrary"),
        cost_estimate=pl.CostEstimate(
            flops=20 * groups * tiles * rows * length * LANES,
            bytes_accessed=query.size * 10 + kv.size * 6,
            transcendentals=groups * tiles * 2 * rows * length,
        ),
        name="prompt_backward",
    )(start, query, kv, out, grad, lse)


def cont_backward_kernel(
    which,
    q_ref,
    kv_ref,
    own_ref,
    o_ref,
    g_ref,
    lse_ref,
    dq_ref,
    dk_ref,
    dv_ref,
    ek_ref,
    ev_ref,
    kt_ref,
    ot_ref,
):
    tile = pl.program_id(1)
    rows = q_ref.shape[1]
    head = tile // (pl.num_programs(1) // 2)

    @pl.when(tile == 0)
    def _():
        kt_ref[...] = kv_ref[0, :, :LANES].astype(F32).T.astype(BF)
        ot_ref[...] = own_ref[0, :, :LANES].astype(F32).T.astype(BF)

    place = pl.ds(pl.multiple_of(head * HEAD_SIZE, HEAD_SIZE), HEAD_SIZE)
    query, grad = q_ref[0], g_ref[0]
    mixed = (grad.astype(F32) * o_ref[0].astype(F32)).T
    delta = jnp.concatenate(
        [
            jnp.sum(mixed[j * HEAD_SIZE : (j + 1) * HEAD_SIZE], axis=0, keepdims=True)
            for j in range(2)
        ],
        axis=1,
    )
    queries = jnp.concatenate([half_of(query, 0), half_of(query, 1)], axis=0)
    grads = jnp.concatenate([half_of(grad, 0), half_of(grad, 1)], axis=0)
    bias = causal_bias(rows, rows, 0)
    lse = lse_ref[0, 0]
    dk, dv, dq = backward_columns(
        doubled(kv_ref[0, :, :LANES], head),
        doubled(kv_ref[0, :, LANES:], head),
        kt_ref[place, :],
        None,
        queries,
        grads,
        lse,
        delta,
        256,
    )
    ek, ev, eq = backward_columns(
        doubled(own_ref[0, :, :LANES], head),
        doubled(own_ref[0, :, LANES:], head),
        ot_ref[place, :],
        jnp.concatenate([bias, bias], axis=1),
        queries,
        grads,
        lse,
        delta,
        rows,
    )
    dq = dq + eq
    dq_ref[0] = jnp.concatenate([dq[:, :rows], dq[:, rows:]], axis=0).T * SCORE_SCALE
    add_into(dk_ref, folded(dk, head) * SCORE_SCALE, tile == 0)
    add_into(dv_ref, folded(dv, head), tile == 0)
    add_into(ek_ref, folded(ek, head) * SCORE_SCALE, tile == 0)
    add_into(ev_ref, folded(ev, head), tile == 0)


def cont_backward(query, kv, own, out, grad, lse, which):
    conts, rows, query_width = query.shape
    length = kv.shape[1]
    tiles = query_width // LANES
    q_spec = pl.BlockSpec((1, rows, LANES), lambda g, t, w: (g, 0, t))
    k_spec = pl.BlockSpec((1, length, LANES), lambda g, t, w: (g, 0, 0))
    e_spec = pl.BlockSpec((1, rows, LANES), lambda g, t, w: (g, 0, 0))
    return pl.pallas_call(
        cont_backward_kernel,
        out_shape=[jax.ShapeDtypeStruct(query.shape, F32)]
        + [jax.ShapeDtypeStruct((conts, length, LANES), F32)] * 2
        + [jax.ShapeDtypeStruct((conts, rows, LANES), F32)] * 2,
        grid_spec=pltpu.PrefetchScalarGridSpec(
            num_scalar_prefetch=1,
            grid=(conts, tiles),
            in_specs=[
                q_spec,
                pl.BlockSpec((1, length, 2 * LANES), lambda g, t, w: (w[g], 0, 0)),
                pl.BlockSpec((1, rows, 2 * LANES), lambda g, t, w: (g, 0, 0)),
                q_spec,
                q_spec,
                pl.BlockSpec((1, 1, 1, 2 * rows), lambda g, t, w: (g, t, 0, 0)),
            ],
            out_specs=[q_spec, k_spec, k_spec, e_spec, e_spec],
            scratch_shapes=[pltpu.VMEM((LANES, length), BF), pltpu.VMEM((LANES, rows), BF)],
        ),
        compiler_params=params_of("arbitrary", "arbitrary"),
        cost_estimate=pl.CostEstimate(
            flops=20 * conts * tiles * rows * (length + rows) * LANES,
            bytes_accessed=query.size * 10 + conts * length * LANES * 12,
            transcendentals=conts * tiles * 2 * rows * (length + rows),
        ),
        name="cont_backward",
    )(which, query, kv, own, out, grad, lse)


def finish_kernel(count, dq_ref, dkv_ref, *refs):
    others = refs[:count]
    q_ref, kv_ref, cosine, sine, out_ref, total_ref = refs[count:]
    query_width = dq_ref.shape[1]
    key_width = dkv_ref.shape[1] // 2
    dkv = dkv_ref[...]
    for other in others:
        dkv = dkv + other[...].astype(F32)
    dq = dq_ref[...]
    total_ref[...] = jnp.sum(dq * q_ref[...].astype(F32), axis=1, keepdims=True) + jnp.sum(
        dkv * kv_ref[...].astype(F32), axis=1, keepdims=True
    )
    back = -sine[...]
    for t in range(query_width // LANES):
        cut = slice(t * LANES, (t + 1) * LANES)
        out_ref[:, cut] = turn(dq[:, cut], cosine[...], back).astype(BF)
    out_ref[:, query_width : query_width + key_width] = turn(
        dkv[:, :key_width], cosine[...], back
    ).astype(BF)
    out_ref[:, query_width + key_width :] = dkv[:, key_width:].astype(BF)


def finish(dq, dkv, others, query, kv, tables):
    rows, query_width = dq.shape
    kv_width = dkv.shape[1]
    block = min(rows, 256)
    row = lambda w: pl.BlockSpec((block, w), lambda i: (i, 0))
    return pl.pallas_call(
        functools.partial(finish_kernel, len(others)),
        out_shape=[
            jax.ShapeDtypeStruct((rows, query_width + kv_width), BF),
            jax.ShapeDtypeStruct((rows, 1), F32),
        ],
        grid=(rows // block,),
        in_specs=[row(query_width)]
        + [row(kv_width)] * (1 + len(others))
        + [row(query_width), row(kv_width), row(LANES), row(LANES)],
        out_specs=[row(query_width + kv_width), row(1)],
        compiler_params=params_of("arbitrary"),
        cost_estimate=pl.CostEstimate(
            flops=20 * dq.size, bytes_accessed=dq.size * 12, transcendentals=0
        ),
        name="finish",
    )(dq, dkv, *others, query, kv, *tables)


def rope_tables(positions):
    lane = jnp.arange(LANES)
    half = HEAD_SIZE // 2
    frequency = ROPE_BASE ** (-(lane % half).astype(F32) * 2.0 / HEAD_SIZE)
    angles = positions.astype(F32)[:, None] * frequency[None, :]
    sign = jnp.where(lane % HEAD_SIZE < half, -1.0, 1.0)
    return jnp.cos(angles), jnp.sin(angles) * sign[None, :]


def second_norm_kernel(count, model_width, order, *refs):
    x, o = refs[:count], refs[count : 2 * count]
    gain, weight, out_ref, hidden_ref, scale_ref = refs[2 * count :]
    width, head_width = x[0].shape[1], o[0].shape[1]
    total = None
    for r, part in enumerate(o):
        term = dot_nn(part[...], weight[r * head_width : (r + 1) * head_width, :])
        total = term if total is None else total + term
    hidden_ref[...] = total
    places = [pl.ds(pl.multiple_of(order[r] * width, width), width) for r in range(count)]
    squares = 0.0
    for place, part in zip(places, x):
        h = hidden_ref[:, place] + part[...].astype(F32)
        hidden_ref[:, place] = h
        squares = squares + jnp.sum(h * h, axis=1, keepdims=True)
    scale = lax.rsqrt(squares / model_width + EPSILON)
    scale_ref[...] = scale
    for r, place in enumerate(places):
        out_ref[:, place] = (hidden_ref[:, place] * scale * gain[r : r + 1, :]).astype(BF)


def spread_kernel(count, order, *refs):
    parts = refs[:count]
    mix, out_ref = refs[count:]
    width = parts[0].shape[1]
    for r, part in enumerate(parts):
        place = pl.ds(pl.multiple_of(order[r] * width, width), width)
        out_ref[:, place] = (part[...].astype(F32) * mix[...]).astype(BF)


def third_norm_kernel(count, model_width, order, *refs):
    cot, n = refs[:count], refs[count : 2 * count]
    gain, scale_ref, mix, hidden_ref, out_ref, factor_ref = refs[2 * count :]
    width = cot[0].shape[1]
    places = [pl.ds(pl.multiple_of(order[r] * width, width), width) for r in range(count)]
    scale = scale_ref[...]
    total = 0.0
    for r, place in enumerate(places):
        total = total + jnp.sum(
            hidden_ref[:, place] * gain[r : r + 1, :] * n[r][...].astype(F32),
            axis=1,
            keepdims=True,
        )
    factor = scale * scale * scale * total / model_width
    factor_ref[...] = factor
    for r, place in enumerate(places):
        value = (
            cot[r][...].astype(F32) * mix[...]
            + scale * gain[r : r + 1, :] * n[r][...].astype(F32)
            - hidden_ref[:, place] * factor
        )
        out_ref[:, place] = value.astype(BF)


def placed_call(kernel, name, order, part_sets, wholes, columns_in, outs, flops=0):
    parts = [p for group in part_sets for p in group]
    rows, width = parts[0].shape
    block = min(rows, 256)
    row = lambda w: pl.BlockSpec((block, w), lambda i, o: (i, 0))
    return pl.pallas_call(
        kernel,
        out_shape=[jax.ShapeDtypeStruct((rows, w), d) for w, d in outs],
        grid_spec=pltpu.PrefetchScalarGridSpec(
            num_scalar_prefetch=1,
            grid=(rows // block,),
            in_specs=[row(p.shape[1]) for p in parts]
            + [pl.BlockSpec(w.shape, lambda i, o: (0, 0)) for w in wholes]
            + [row(c.shape[1]) for c in columns_in],
            out_specs=[row(w) for w, d in outs],
        ),
        compiler_params=params_of("arbitrary"),
        cost_estimate=pl.CostEstimate(
            flops=8 * len(parts) * rows * width + flops,
            bytes_accessed=2 * len(parts) * rows * width,
            transcendentals=rows,
        ),
        name=name,
    )(order, *parts, *wholes, *columns_in)


def second_norm(x, o, gains, weight, order):
    count, width = len(x), x[0].shape[1]
    return placed_call(
        functools.partial(second_norm_kernel, count, count * width),
        "second_norm",
        order,
        [x, o],
        [gains, weight],
        [],
        [(count * width, BF), (count * width, F32), (1, F32)],
        x[0].shape[0] * weight.size * 2,
    )


def spread(parts, mix, order):
    count, width = len(parts), parts[0].shape[1]
    return placed_call(
        functools.partial(spread_kernel, count),
        "spread",
        order,
        [parts],
        [],
        [mix],
        [(count * width, BF)],
    )[0]


def third_norm(hidden, cot, n, gains, scale, mix, order):
    count, width = len(cot), cot[0].shape[1]
    return placed_call(
        functools.partial(third_norm_kernel, count, count * width),
        "third_norm",
        order,
        [cot, n],
        [gains],
        [scale, mix, hidden],
        [(count * width, BF), (1, F32)],
    )


def body(
    prompt_in,
    cont_in,
    prompt_mask,
    cont_mask,
    cont_prompt,
    cont_start,
    gain_attn,
    gain_ffn,
    router,
    w_query,
    key_projection,
    w_value,
    w_out,
    w_gate,
    w_up,
    w_down,
    prompt_cot,
    cont_cot,
):
    groups, prompt_rows, width = prompt_in.shape
    conts = cont_in.shape[0]
    tp_size = lax.axis_size("tp")
    ctx_size = lax.axis_size("ctx")
    model_width = width * tp_size
    me_tp = lax.axis_index("tp")
    me_ctx = lax.axis_index("ctx")
    query_width = w_query.shape[1]
    key_width = key_projection.shape[1]
    kv_width = 2 * key_width
    streams = range(2)
    tokens_in = [prompt_in.reshape(-1, width), cont_in.reshape(-1, width)]
    cots = [prompt_cot.reshape(-1, width), cont_cot.reshape(-1, width)]
    masks = [prompt_mask.reshape(-1, 1).astype(F32), cont_mask.reshape(-1, 1).astype(F32)]
    prompt_place = me_ctx * prompt_rows + jnp.arange(prompt_rows, dtype=jnp.int32)
    cont_place = (
        cont_start[:, None] + jnp.arange(CONTINUATION_LEN, dtype=jnp.int32)[None, :]
    ).reshape(-1)
    tables = [rope_tables(jnp.tile(prompt_place, groups)), rope_tables(cont_place)]
    local_prompt = jnp.clip(cont_prompt - lax.axis_index("fsdp") * groups, 0, groups - 1)
    start = (me_ctx * prompt_rows).astype(jnp.int32)[None]
    order = jnp.stack([me_tp ^ step for step in range(tp_size)]).astype(jnp.int32)

    qkv_moves, lay_qkv = gather_weight(
        jnp.concatenate([w_query, key_projection, w_value], axis=1), 0
    )
    x_prompt, sent_prompt = gather_tp(tokens_in[0], qkv_moves[0])
    full_qkv = lay_qkv(None)
    small_params = tie(jnp.stack([gain_attn, gain_ffn, router]), x_prompt[2])
    params = [p.astype(F32) for p in pieces_of(small_params)]
    gains_attn = jnp.stack([p[0] for p in params])
    gains_ffn = jnp.stack([p[1] for p in params])
    routers = jnp.stack([p[2] for p in params])
    gate_moves, lay_gate = gather_weight(w_gate, 0, qkv_moves[0])
    up_moves, lay_up = gather_weight(w_up, 0, gate_moves[0])
    down_moves, lay_down = gather_weight(w_down, 1, up_moves[0])
    sent_out, out_moves, lay_out = gather_out(w_out, sent_prompt)
    x_cont, sent_cont = gather_tp(tie(tokens_in[1], sent_out))
    x_parts = [x_prompt, tie(x_cont, out_moves[1])]

    def enter(i):
        return entry(
            x_parts[i], gains_attn, routers, full_qkv, masks[i], tables[i], order, query_width
        )

    xn1, query, kv, scale_attn, gate_router, mixing = zip(enter(0), enter(1))
    own_kv = kv[0].reshape(groups, prompt_rows, kv_width)
    prompt_kv = jnp.zeros((groups, prompt_rows * ctx_size, kv_width), BF)
    for step, part in enumerate(pieces_of(own_kv, "ctx")):
        prompt_kv = lax.dynamic_update_slice(prompt_kv, part, (0, (me_ctx ^ step) * prompt_rows, 0))
    query = [tie(query[0], (sent_out, up_moves[0])), tie(query[1], (gate_moves[1], down_moves[0]))]
    full_out = lay_out(xn1[0])
    full_gate = lay_gate(xn1[0])
    full_up = lay_up(xn1[1])
    full_down = lay_down(xn1[1])
    queries = [
        query[0].reshape(groups, prompt_rows, query_width),
        query[1].reshape(conts, CONTINUATION_LEN, query_width),
    ]
    cont_kv = kv[1].reshape(conts, CONTINUATION_LEN, kv_width)
    prompt_o, prompt_lse = prompt_forward(queries[0], prompt_kv, start)
    cont_o, cont_lse = cont_forward(queries[1], prompt_kv, cont_kv, local_prompt)
    attended = [prompt_o.reshape(-1, query_width), cont_o.reshape(-1, query_width)]
    o_prompt, sent_prompt = gather_tp(attended[0])
    o_cont, sent_cont = gather_tp(
        tie(attended[1], (sent_prompt, out_moves, up_moves[1]))
    )

    def second(i, o):
        return second_norm(x_parts[i], o, gains_ffn, full_out, order)

    xn2_prompt, hidden_prompt, scale_prompt = second(0, o_prompt)
    cot_cont, sent_cont = gather_tp(tie(cots[1], sent_cont))
    xn2_cont, hidden_cont, scale_cont = second(1, o_cont)
    xn2, hidden, scale_ffn = (
        [xn2_prompt, xn2_cont],
        [hidden_prompt, hidden_cont],
        [scale_prompt, scale_cont],
    )

    def forward(i):
        g = product(xn2[i], full_gate)
        u = product(xn2[i], full_up)
        s = jax.nn.sigmoid(g)
        return g, u, s, (g * s * u).astype(BF)

    ahead = [forward(0), forward(1)]
    cot_prompt, sent_prompt = gather_tp(tie(cots[0], (sent_cont, ahead[0][3], xn2_cont, down_moves[1])))
    cot_parts = [cot_prompt, cot_cont]

    inner, gate_grad, up_grad = [None, None], [None, None], [None, None]
    ffn_grad, blocks = [None, None], [None, None]
    for i in (1, 0):
        g, u, s, inner[i] = ahead[i]
        mix = mixing[i] if i == 1 else tie(mixing[i], blocks[1])
        ffn_grad[i] = spread(cot_parts[i], mix, order)
        dz = product_nt(ffn_grad[i], full_down)
        gate_grad[i] = (dz * u * s * (1.0 + g * (1.0 - s))).astype(BF)
        up_grad[i] = (dz * g * s).astype(BF)
        blocks[i] = blocks_of(
            lambda b, i=i: product_nt(gate_grad[i], rows_of(full_gate, b, width))
            + product_nt(up_grad[i], rows_of(full_up, b, width))
        )
        if i == 1:
            cont_sum, sent_cont = exchange_direct(blocks[1])

    both = lambda pair: jnp.concatenate(pair, axis=0)
    normed_grad = [None, cont_sum]
    blocks[0] = tie(blocks[0], cont_sum)
    normed_grad[0], sent_prompt = exchange_direct(blocks[0])
    n_cont = pieces_of(normed_grad[1].astype(BF))
    xn2_all, gate_all, up_all, inner_all, ffn_grad_all = tie(
        (both(xn2), both(gate_grad), both(up_grad), both(inner), both(ffn_grad)), blocks[0]
    )
    parts = [
        product_tn(xn2_all, gate_all).astype(BF),
        product_tn(xn2_all, up_all).astype(BF),
        product_tn(inner_all, ffn_grad_all).astype(BF),
    ]
    pieces = [scatter_grad(part, axis) for part, axis in zip(parts, (0, 0, 1))]
    late = tie(normed_grad[0].astype(BF), (n_cont, parts))
    n_prompt = pieces_of(late)
    n_parts = [n_prompt, n_cont]
    inner_late = tie(inner, parts)
    ffn_blocks = [
        blocks_of(lambda b, t=t: product(t, columns(full_down, b, width))) for t in inner_late
    ]

    def third(i):
        return third_norm(
            hidden[i], cot_parts[i], n_parts[i], gains_ffn, scale_ffn[i], mixing[i], order
        )

    dab_cont, factor_cont = third(1)
    do_cont = product_nt(dab_cont, full_out[:query_width]).astype(BF)
    dq_cont, dk_cont, dv_cont, dk_own, dv_own = cont_backward(
        queries[1],
        prompt_kv,
        cont_kv,
        cont_o,
        do_cont.reshape(queries[1].shape),
        cont_lse,
        local_prompt,
    )
    dab_prompt, factor_prompt = third(0)
    do_prompt = product_nt(dab_prompt, full_out[:query_width]).astype(BF)
    dab, factor = [dab_prompt, dab_cont], [factor_prompt, factor_cont]
    ffn_blocks = tie(ffn_blocks, n_prompt)
    branch_ffn = [None, None]
    branch_ffn[1], sent_cont = exchange_direct(ffn_blocks[1])
    branch_ffn[0], sent_prompt = exchange_direct(ffn_blocks[0])
    across = [swap(p, "ctx", 2) if paired() else p for p in pieces]
    dq_prompt, dk_prompt, dv_prompt = prompt_backward(
        queries[0], prompt_kv, prompt_o, do_prompt.reshape(queries[0].shape), prompt_lse, start
    )
    dq_prompt = tie(dq_prompt, branch_ffn[1])
    started_out = grad_start(both(attended), tie(both(dab), dq_prompt), 1)
    chosen = (local_prompt[:, None] == jnp.arange(groups, dtype=jnp.int32)[None, :]).astype(F32)

    def kv_block(step):
        place = (me_ctx ^ step) * prompt_rows

        def piece(whole):
            return lax.dynamic_slice(
                whole, (0, place, 0), (whole.shape[0], prompt_rows, whole.shape[2])
            )

        def total(prompts, extra):
            extra = piece(extra)
            sums = [
                sum(chosen[c, g] * extra[c] for c in range(conts)) for g in range(groups)
            ]
            return piece(prompts) + jnp.stack(sums)

        return jnp.concatenate(
            [total(dk_prompt, dk_cont), total(dv_prompt, dv_cont)], axis=2
        ).reshape(-1, kv_width)

    sent = [swap(kv_block(step).astype(BF), "ctx", step) for step in range(1, ctx_size)]
    dkv_own = jnp.concatenate([dk_own, dv_own], axis=2).reshape(-1, kv_width)
    finished_cont = finish(
        dq_cont.reshape(-1, query_width), dkv_own, [], query[1], kv[1], tables[1]
    )
    finished = [
        finish(dq_prompt.reshape(-1, query_width), kv_block(0), sent, query[0], kv[0], tables[0]),
        finished_cont,
    ]
    dqkv = [f[0] for f in finished]
    attn_blocks = [
        blocks_of(lambda b, t=t: product_nt(t, rows_of(full_qkv, b, width))) for t in dqkv
    ]
    qkv_left, qkv_right = tie((both(xn1), both(dqkv)), attn_blocks)
    started_qkv = grad_start(qkv_left, qkv_right, 0)
    normed_attn_grad = [None, None]
    normed_attn_grad[1], relay_cont, _ = exchange_sum(
        tie(attn_blocks[1], sent_prompt), across[0]
    )
    sizes = [t.shape[0] for t in dqkv]
    joined = lambda pair: jnp.concatenate([p.reshape(-1, LANES) for p in pair], axis=0)
    parted = lambda t: [
        p.reshape(-1, 1) for p in jnp.split(t, [sizes[0] // LANES], axis=0)
    ]
    total_attn = parted(all_sum(joined([f[1] for f in finished])))
    grad_out = grad_end(grad_middle(*started_out, 1), 1)
    grad_qkv = grad_end(grad_middle(*started_qkv, 0), 0)
    grad_gate, grad_up, grad_down = [
        spread_grad(piece, far, axis) for piece, far, axis in zip(pieces, across, (0, 0, 1))
    ]

    gain_attn_sum, gain_ffn_sum, router_sum = 0.0, 0.0, 0.0
    outs, token_grads = [], []
    hidden_own = [columns(h, me_tp, width) for h in hidden]
    branch = [
        hidden_own[i] - tokens_in[i].astype(F32) + branch_ffn[i] for i in streams
    ]
    sums = parted(
        all_sum(
            joined(
                [
                    jnp.sum(cots[i].astype(F32) * mixing[i] * branch[i], axis=1, keepdims=True)
                    for i in streams
                ]
            )
        )
    )
    normed_attn_grad[0] = exchange_sum(
        tie(attn_blocks[0], (relay_cont, branch_ffn[0])),
        (sums, total_attn, across[1]),
    )[0]
    for i in streams:
        x = tokens_in[i].astype(F32)
        dy = cots[i].astype(F32)
        outs.append((x + mixing[i] * branch[i]).astype(BF))
        dl = (1.0 - gate_router[i]) * sums[i]
        router_sum = router_sum + jnp.sum(x * dl, axis=0)
        gain_ffn_sum = gain_ffn_sum + jnp.sum(
            hidden_own[i] * scale_ffn[i] * normed_grad[i], axis=0
        )
        back_ffn = scale_ffn[i] * gains_ffn[0:1] * normed_grad[i] - hidden_own[i] * factor[i]
        scale = scale_attn[i]
        n = normed_attn_grad[i]
        gain_attn_sum = gain_attn_sum + jnp.sum(x * scale * n, axis=0)
        n1 = scale * gains_attn[0:1] * n - x * (scale * scale * total_attn[i] / model_width)
        token_grads.append(dy + dl * routers[0:1] + back_ffn + n1)
    small = group_sum(jnp.stack([gain_attn_sum, gain_ffn_sum, router_sum]))
    return (
        outs[0].reshape(prompt_in.shape),
        outs[1].reshape(cont_in.shape),
        token_grads[0].reshape(prompt_in.shape),
        token_grads[1].reshape(cont_in.shape),
        small[0],
        small[1],
        small[2],
        grad_qkv[:, :query_width],
        grad_qkv[:, query_width : query_width + key_width],
        grad_qkv[:, query_width + key_width :],
        grad_out,
        grad_gate,
        grad_up,
        grad_down,
    )


def solution(mesh):
    placed = (
        P("fsdp", "ctx", "tp"),
        P(("fsdp", "ctx"), None, "tp"),
        P("fsdp", "ctx"),
        P(("fsdp", "ctx"), None),
        P(("fsdp", "ctx")),
        P(("fsdp", "ctx")),
        P("tp"),
        P("tp"),
        P("tp"),
        P("fsdp", "tp"),
        P("fsdp", "tp"),
        P("fsdp", "tp"),
        P("tp", "fsdp"),
        P("fsdp", "tp"),
        P("fsdp", "tp"),
        P("tp", "fsdp"),
        P("fsdp", "ctx", "tp"),
        P(("fsdp", "ctx"), None, "tp"),
    )
    return jax.shard_map(
        body,
        mesh=mesh,
        in_specs=placed,
        out_specs=(
            P("fsdp", "ctx", "tp"),
            P(("fsdp", "ctx"), None, "tp"),
            P("fsdp", "ctx", "tp"),
            P(("fsdp", "ctx"), None, "tp"),
            P("tp"),
            P("tp"),
            P("tp"),
            P("fsdp", "tp"),
            P("fsdp", "tp"),
            P("fsdp", "tp"),
            P("tp", "fsdp"),
            P("fsdp", "tp"),
            P("fsdp", "tp"),
            P("tp", "fsdp"),
        ),
        check_vma=False,
    )
```

```python
import functools

import jax
import jax.numpy as jnp
from jax import lax
from jax.experimental import pallas as pl
from jax.experimental.pallas import tpu as pltpu
from jax.sharding import PartitionSpec as P

HEAD_SIZE = 64
CONTINUATION_LEN = 128
EPSILON = 1e-05
ROPE_BASE = 500000.0
BF = jnp.bfloat16
F32 = jnp.float32
EVERY = ("fsdp", "ctx")


def product(left, right):
    return jnp.dot(left, right, preferred_element_type=F32)


def product_nt(left, right):
    return lax.dot_general(left, right, (((1,), (1,)), ((), ())), preferred_element_type=F32)


def product_tn(left, right):
    return lax.dot_general(left, right, (((0,), (0,)), ((), ())), preferred_element_type=F32)


def swap(value, axis, step):
    count = lax.axis_size(axis)
    return lax.ppermute(value, axis, [(i, i ^ step) for i in range(count)])


def pieces_of(value, axis="tp"):
    return [value] + [swap(value, axis, step) for step in range(1, lax.axis_size(axis))]


def tie(values, deps):
    return lax.optimization_barrier((values, deps))[0]


def inner_pair():
    me = lax.axis_index("tp")
    return (me == 1) | (me == 2)


def gather_tp(value, before=None):
    if lax.axis_size("tp") != 4:
        parts = pieces_of(value)
        return parts, parts[1:]
    second = swap(value, "tp", 2)
    first = swap(value, "tp", 1)
    middle = lax.ppermute(value, "tp", [(1, 2), (2, 1)])
    ready = tie(second, first if before is None else (first, before))
    passed = lax.ppermute(ready, "tp", [(2, 3), (1, 0)])
    third = jnp.where(inner_pair(), middle, passed)
    return [value, first, second, third], [first, second, middle, passed]


def all_sum(value, axis="tp"):
    parts = pieces_of(value, axis)
    total = parts[0]
    for part in parts[1:]:
        total = total + part
    return total


def group_sum(value):
    if not paired():
        return lax.psum(value, EVERY)
    value = all_sum(value, "ctx")
    return value + swap(value, "fsdp", 1)


def blocks_of(make_block):
    me = lax.axis_index("tp")
    blocks = [make_block(me ^ step) for step in range(lax.axis_size("tp"))]
    if len(blocks) != 4:
        return [blocks[0]] + [block.astype(BF) for block in blocks[1:]]
    return [blocks[0], blocks[1].astype(BF), blocks[2], blocks[3].astype(BF)]


def exchange_direct(blocks):
    sent = [swap(block.astype(BF), "tp", step) for step, block in enumerate(blocks) if step > 0]
    total = blocks[0]
    for part in sent:
        total = total + part.astype(F32)
    return total, sent


def exchange_sum(blocks, after=()):
    if len(blocks) != 4:
        sent = [swap(block, "tp", step) for step, block in enumerate(blocks) if step > 0]
        early, phase = sent[0], sent
    else:
        passed = lax.ppermute(blocks[3], "tp", [(3, 2), (0, 1)])
        middle = lax.ppermute(blocks[3], "tp", [(1, 2), (2, 1)])
        first = swap(blocks[1], "tp", 1)
        phase = [passed, middle, first]
        passed, middle, first = tie(phase, after)
        early = (blocks[2] + passed.astype(F32)).astype(BF)
        sent = [middle, first, swap(early, "tp", 2)]
    total = blocks[0]
    for part in sent:
        total = total + part.astype(F32)
    return total, early, phase


def columns(matrix, block, width):
    return lax.dynamic_slice(matrix, (0, block * width), (matrix.shape[0], width))


def rows_of(matrix, block, width):
    return lax.dynamic_slice(matrix, (block * width, 0), (width, matrix.shape[1]))


def cut_of(matrix, axis, block, width):
    return rows_of(matrix, block, width) if axis == 0 else columns(matrix, block, width)


def paired():
    return lax.axis_size("fsdp") == 2 and lax.axis_size("ctx") == 4


def gather_weight(weight, axis, after=None):
    me = lax.axis_index("ctx")
    size = weight.shape[axis] // lax.axis_size("ctx")
    if not paired():
        quarter = cut_of(weight, axis, me, size)
        return [quarter] * 2, lambda after: lax.all_gather(quarter, EVERY, axis=axis, tiled=True)
    if after is not None:
        weight = tie(weight, after)
    mine = lax.axis_index("fsdp")
    far = swap(cut_of(weight, axis, me, size), "fsdp", 1)
    across = swap(far, "ctx", 2)
    found = [(0, far), (2, across), (1, swap(far, "ctx", 1)), (3, swap(across, "ctx", 1))]
    shape = list(weight.shape)
    shape[axis] *= 2
    at = lambda start: (start, 0) if axis == 0 else (0, start)

    def whole(after):
        own = weight if after is None else tie(weight, after)
        result = lax.dynamic_update_slice(
            jnp.zeros(shape, weight.dtype), own, at(mine * size * 4)
        )
        for step, part in found:
            result = lax.dynamic_update_slice(
                result, part, at(((1 - mine) * 4 + (me ^ step)) * size)
            )
        return result

    return [far, across], whole


def gather_out(weight, after):
    if not paired():
        pieces, done = gather_tp(lax.all_gather(weight, "fsdp", axis=1, tiled=True))
        return done, pieces, lambda after: jnp.concatenate(pieces, axis=0)
    me = lax.axis_index("ctx")
    mine = lax.axis_index("fsdp")
    size = weight.shape[1] // lax.axis_size("ctx")
    pieces, done = gather_tp(tie(columns(weight, me, size), after))
    own = jnp.concatenate(pieces, axis=0)
    far = swap(own, "fsdp", 1)
    across = swap(own, "ctx", 2)
    far_across = swap(across, "fsdp", 1)
    found = [(mine, 0, own), (1 - mine, 0, far), (mine, 2, across), (1 - mine, 2, far_across)]
    found += [(f, step ^ 1, swap(part, "ctx", 1)) for f, step, part in found]

    def whole(after):
        result = jnp.zeros((own.shape[0], size * 8), weight.dtype)
        for f, step, part in found:
            result = lax.dynamic_update_slice(result, part, (0, (f * 4 + (me ^ step)) * size))
        return result

    return done, [far, across, far_across], whole


def scatter_grad(part, axis):
    return lax.psum_scatter(part, EVERY, scatter_dimension=axis, tiled=True)


def spread_grad(piece, across, axis):
    if not paired():
        return lax.all_gather(piece, "ctx", axis=axis, tiled=True).astype(F32)
    low_side = lax.axis_index("ctx") // 2 == 0
    low_core = lax.axis_index("ctx") % 2 == 0
    pair = [jnp.where(low_side, piece, across), jnp.where(low_side, across, piece)]
    parts = []
    for mine, theirs in zip(pair, [swap(p, "ctx", 1) for p in pair]):
        parts += [jnp.where(low_core, mine, theirs), jnp.where(low_core, theirs, mine)]
    return jnp.concatenate(parts, axis=axis).astype(F32)


def grad_start(left, right, axis):
    if not paired():
        whole = product_tn(left, right).astype(BF)
        return whole, whole, whole
    mine = lax.axis_index("fsdp")
    core = lax.axis_index("ctx") % 2
    split, other = (left, right) if axis == 0 else (right, left)
    half = lambda m, i: columns(m, i, m.shape[1] // 2)
    split_far, split_own = half(split, 1 - mine), half(split, mine)
    other_far, other_own = half(other, 1 - core), half(other, core)
    dot = lambda s, t: product_tn(s, t) if axis == 0 else product_tn(t, s)
    first = swap(dot(split_far, other_far).astype(BF), "ctx", 1)
    far = (dot(split_far, other_own) + first.astype(F32)).astype(BF)
    split_own = tie(split_own, far)
    second = swap(dot(split_own, other_far).astype(BF), "ctx", 1)
    kept = dot(split_own, other_own) + second.astype(F32)
    return swap(far, "fsdp", 1), kept, far


def grad_middle(arrived, kept, far, axis):
    if not paired():
        return lax.psum_scatter(kept, EVERY, scatter_dimension=axis, tiled=True)
    side = lax.axis_index("ctx") // 2
    size = kept.shape[axis] // 2
    half = lambda i: cut_of(kept, axis, i, size) + cut_of(arrived, axis, i, size).astype(F32)
    sent = swap(half(1 - side).astype(BF), "ctx", 2)
    return (half(side) + sent.astype(F32)).astype(BF)


def grad_end(piece, axis):
    if not paired():
        return lax.all_gather(piece, "ctx", axis=axis, tiled=True).astype(F32)
    side = lax.axis_index("ctx") // 2
    core = lax.axis_index("ctx") % 2
    across = swap(piece, "ctx", 2)
    own = in_order(piece, across, side, axis)
    return in_order(own, swap(own, "ctx", 1), core, 1 - axis).astype(F32)


def in_order(mine, theirs, index, axis):
    low = index == 0
    return jnp.concatenate(
        [jnp.where(low, mine, theirs), jnp.where(low, theirs, mine)], axis=axis
    )


LOG2E = 1.4426950408889634
SCORE_SCALE = 0.125
LANES = 128


def lane_index(shape):
    return lax.broadcasted_iota(jnp.int32, shape, len(shape) - 1)


def turn(tile, cosine, sine):
    low = lane_index(tile.shape) % HEAD_SIZE < HEAD_SIZE // 2
    other = jnp.where(
        low,
        pltpu.roll(tile, LANES - HEAD_SIZE // 2, 1),
        pltpu.roll(tile, HEAD_SIZE // 2, 1),
    )
    return tile * cosine + other * sine


def doubled(tile, head):
    wide = tile.astype(F32)
    low = lane_index(tile.shape) < HEAD_SIZE
    other = pltpu.roll(wide, HEAD_SIZE, 1)
    return jnp.where(low == (head == 0), wide, other).astype(tile.dtype)


def half_of(tile, j):
    low = lane_index(tile.shape) < HEAD_SIZE
    keep = low if j == 0 else jnp.logical_not(low)
    return jnp.where(keep, tile, jnp.zeros_like(tile))


def dot_nt(left, right):
    return lax.dot_general(left, right, (((1,), (1,)), ((), ())), preferred_element_type=F32)


def dot_nn(left, right):
    return lax.dot_general(left, right, (((1,), (0,)), ((), ())), preferred_element_type=F32)


def params_of(*semantics, limit=56 << 20):
    return pltpu.CompilerParams(dimension_semantics=semantics, vmem_limit_bytes=limit)


def entry_kernel(count, model_width, query_width, order, *refs):
    parts = refs[:count]
    gain, router, weight, mask, cosine, sine = refs[count : count + 6]
    xn_ref, query_ref, kv_ref, scale_ref, gate_ref, mix_ref = refs[count + 6 :]
    width = parts[0].shape[1]
    wide = [p[...].astype(F32) for p in parts]
    squares = sum(jnp.sum(w * w, axis=1, keepdims=True) for w in wide)
    logits = sum(
        jnp.sum(w * router[r : r + 1, :], axis=1, keepdims=True) for r, w in enumerate(wide)
    )
    scale = lax.rsqrt(squares / model_width + EPSILON)
    gate = jax.nn.sigmoid(logits)
    scale_ref[...] = scale
    gate_ref[...] = gate
    mix_ref[...] = mask[...] * gate
    total = None
    for r, w in enumerate(wide):
        normed = (w * scale * gain[r : r + 1, :]).astype(BF)
        place = pl.ds(pl.multiple_of(order[r] * width, width), width)
        xn_ref[:, place] = normed
        term = dot_nn(normed, weight[place, :])
        total = term if total is None else total + term
    for t in range(query_width // LANES):
        cut = slice(t * LANES, (t + 1) * LANES)
        query_ref[:, cut] = turn(total[:, cut], cosine[...], sine[...]).astype(BF)
    key_width = kv_ref.shape[1] // 2
    key = total[:, query_width : query_width + key_width]
    kv_ref[:, :key_width] = turn(key, cosine[...], sine[...]).astype(BF)
    kv_ref[:, key_width:] = total[:, query_width + key_width :].astype(BF)


def entry(parts, gains, routers, weight, mask, tables, order, query_width):
    rows, width = parts[0].shape
    count = len(parts)
    block = min(rows, 256)
    total_width = weight.shape[1]
    kv_width = total_width - query_width
    whole = lambda a: pl.BlockSpec(a.shape, lambda i, o: (0, 0))
    row = lambda w: pl.BlockSpec((block, w), lambda i, o: (i, 0))
    outs = [(width * count, BF), (query_width, BF), (kv_width, BF), (1, F32), (1, F32), (1, F32)]
    return pl.pallas_call(
        functools.partial(entry_kernel, count, width * count, query_width),
        out_shape=[jax.ShapeDtypeStruct((rows, w), d) for w, d in outs],
        grid_spec=pltpu.PrefetchScalarGridSpec(
            num_scalar_prefetch=1,
            grid=(rows // block,),
            in_specs=[row(width)] * count
            + [whole(gains), whole(routers), whole(weight), row(1), row(LANES), row(LANES)],
            out_specs=[row(w) for w, d in outs],
        ),
        compiler_params=params_of("arbitrary"),
        cost_estimate=pl.CostEstimate(
            flops=2 * rows * width * count * total_width,
            bytes_accessed=rows * width * count * 4 + weight.size * 2,
            transcendentals=rows,
        ),
        name="entry",
    )(order, *parts, gains, routers, weight, mask, *tables)


def softmax_columns(keys, biases, queries, scores):
    top = None
    for i, (key, bias) in enumerate(zip(keys, biases)):
        s = dot_nt(key, queries) * (SCORE_SCALE * LOG2E)
        if bias is not None:
            s = s + bias
        scores[i][...] = s
        part = jnp.max(s, axis=0, keepdims=True)
        top = part if top is None else jnp.maximum(top, part)
    total = 0.0
    for ref in scores:
        e = jnp.exp2(ref[...] - top)
        ref[...] = e
        total = total + jnp.sum(e, axis=0, keepdims=True)
    share = 1.0 / total
    return [(ref[...] * share).astype(BF) for ref in scores], top + jnp.log2(total)


def causal_bias(keys, rows, start):
    key = lax.broadcasted_iota(jnp.int32, (keys, rows), 0)
    row = lax.broadcasted_iota(jnp.int32, (keys, rows), 1)
    return jnp.where(key <= row + start, 0.0, -1e30)


def prompt_forward_kernel(start, q_ref, kv_ref, o_ref, lse_ref, vt_ref, bias_ref, s_ref):
    tile = pl.program_id(1)
    rows = q_ref.shape[1]
    head = tile // (pl.num_programs(1) // 2)

    @pl.when((pl.program_id(0) == 0) & (tile == 0))
    def _():
        bias_ref[...] = causal_bias(bias_ref.shape[0], rows, start[0])

    @pl.when(tile == 0)
    def _():
        vt_ref[...] = kv_ref[0, :, LANES:].astype(F32).T.astype(BF)

    key = doubled(kv_ref[0, :, :LANES], head)
    value_t = vt_ref[pl.ds(pl.multiple_of(head * HEAD_SIZE, HEAD_SIZE), HEAD_SIZE), :]
    query = q_ref[0]
    outs = []
    for j in range(2):
        probs, lse = softmax_columns([key], [bias_ref[...]], half_of(query, j), [s_ref])
        lse_ref[0, 0, j : j + 1, :] = lse
        outs.append(dot_nn(value_t, probs[0]))
    o_ref[0] = jnp.concatenate(outs, axis=0).T.astype(BF)


def prompt_forward(query, kv, start):
    groups, rows, query_width = query.shape
    length = kv.shape[1]
    tiles = query_width // LANES
    return pl.pallas_call(
        prompt_forward_kernel,
        out_shape=[
            jax.ShapeDtypeStruct(query.shape, BF),
            jax.ShapeDtypeStruct((groups, tiles, 2, rows), F32),
        ],
        grid_spec=pltpu.PrefetchScalarGridSpec(
            num_scalar_prefetch=1,
            grid=(groups, tiles),
            in_specs=[
                pl.BlockSpec((1, rows, LANES), lambda g, t, s: (g, 0, t)),
                pl.BlockSpec((1, length, 2 * LANES), lambda g, t, s: (g, 0, 0)),
            ],
            out_specs=[
                pl.BlockSpec((1, rows, LANES), lambda g, t, s: (g, 0, t)),
                pl.BlockSpec((1, 1, 2, rows), lambda g, t, s: (g, t, 0, 0)),
            ],
            scratch_shapes=[
                pltpu.VMEM((LANES, length), BF),
                pltpu.VMEM((length, rows), F32),
                pltpu.VMEM((length, rows), F32),
            ],
        ),
        compiler_params=params_of("arbitrary", "arbitrary"),
        cost_estimate=pl.CostEstimate(
            flops=8 * groups * tiles * rows * length * LANES,
            bytes_accessed=query.size * 4 + kv.size * 2,
            transcendentals=groups * tiles * 2 * rows * length,
        ),
        name="prompt_forward",
    )(start, query, kv)


def cont_forward_kernel(which, q_ref, kv_ref, own_ref, o_ref, lse_ref, vt_ref, wt_ref, s_ref, t_ref):
    tile = pl.program_id(1)
    rows = q_ref.shape[1]
    head = tile // (pl.num_programs(1) // 2)

    @pl.when(tile == 0)
    def _():
        vt_ref[...] = kv_ref[0, :, LANES:].astype(F32).T.astype(BF)
        wt_ref[...] = own_ref[0, :, LANES:].astype(F32).T.astype(BF)

    place = pl.ds(pl.multiple_of(head * HEAD_SIZE, HEAD_SIZE), HEAD_SIZE)
    keys = [doubled(kv_ref[0, :, :LANES], head), doubled(own_ref[0, :, :LANES], head)]
    query = q_ref[0]
    both = jnp.concatenate([half_of(query, 0), half_of(query, 1)], axis=0)
    bias = causal_bias(rows, rows, 0)
    probs, lse = softmax_columns(
        keys, [None, jnp.concatenate([bias, bias], axis=1)], both, [s_ref, t_ref]
    )
    out = dot_nn(vt_ref[place, :], probs[0]) + dot_nn(wt_ref[place, :], probs[1])
    lse_ref[0, 0] = lse
    o_ref[0] = jnp.concatenate([out[:, :rows], out[:, rows:]], axis=0).T.astype(BF)


def cont_forward(query, kv, own, which):
    conts, rows, query_width = query.shape
    length = kv.shape[1]
    tiles = query_width // LANES
    return pl.pallas_call(
        cont_forward_kernel,
        out_shape=[
            jax.ShapeDtypeStruct(query.shape, BF),
            jax.ShapeDtypeStruct((conts, tiles, 1, 2 * rows), F32),
        ],
        grid_spec=pltpu.PrefetchScalarGridSpec(
            num_scalar_prefetch=1,
            grid=(conts, tiles),
            in_specs=[
                pl.BlockSpec((1, rows, LANES), lambda g, t, w: (g, 0, t)),
                pl.BlockSpec((1, length, 2 * LANES), lambda g, t, w: (w[g], 0, 0)),
                pl.BlockSpec((1, rows, 2 * LANES), lambda g, t, w: (g, 0, 0)),
            ],
            out_specs=[
                pl.BlockSpec((1, rows, LANES), lambda g, t, w: (g, 0, t)),
                pl.BlockSpec((1, 1, 1, 2 * rows), lambda g, t, w: (g, t, 0, 0)),
            ],
            scratch_shapes=[
                pltpu.VMEM((LANES, length), BF),
                pltpu.VMEM((LANES, rows), BF),
                pltpu.VMEM((length, 2 * rows), F32),
                pltpu.VMEM((rows, 2 * rows), F32),
            ],
        ),
        compiler_params=params_of("arbitrary", "arbitrary"),
        cost_estimate=pl.CostEstimate(
            flops=8 * conts * tiles * rows * (length + rows) * LANES,
            bytes_accessed=query.size * 4 + conts * length * LANES * 4,
            transcendentals=conts * tiles * 2 * rows * (length + rows),
        ),
        name="cont_forward",
    )(which, query, kv, own)


def backward_columns(key, value, key_t, bias, query, grad, lse, delta, chunk):
    dks, dvs, dq = [], [], None
    for c in range(key.shape[0] // chunk):
        cut = slice(c * chunk, (c + 1) * chunk)
        s = dot_nt(key[cut], query) * (SCORE_SCALE * LOG2E)
        if bias is not None:
            s = s + bias[cut]
        p = jnp.exp2(s - lse)
        dp = dot_nt(value[cut], grad)
        ds = (p * (dp - delta)).astype(BF)
        dvs.append(dot_nn(p.astype(BF), grad))
        dks.append(dot_nn(ds, query))
        term = dot_nn(key_t[:, cut], ds)
        dq = term if dq is None else dq + term
    return dks, dvs, dq


def folded(parts, head):
    whole = jnp.concatenate(parts, axis=0)
    low = lane_index(whole.shape) < HEAD_SIZE
    return jnp.where(low == (head == 0), whole + pltpu.roll(whole, HEAD_SIZE, 1), 0.0)


def add_into(ref, value, first):
    @pl.when(first)
    def _():
        ref[0] = value

    @pl.when(jnp.logical_not(first))
    def _():
        ref[0] = ref[0] + value


def prompt_backward_kernel(
    start, q_ref, kv_ref, o_ref, g_ref, lse_ref, dq_ref, dk_ref, dv_ref, kt_ref, bias_ref
):
    tile = pl.program_id(1)
    rows = q_ref.shape[1]
    head = tile // (pl.num_programs(1) // 2)

    @pl.when((pl.program_id(0) == 0) & (tile == 0))
    def _():
        bias_ref[...] = causal_bias(bias_ref.shape[0], rows, start[0])

    @pl.when(tile == 0)
    def _():
        kt_ref[...] = kv_ref[0, :, :LANES].astype(F32).T.astype(BF)

    key = doubled(kv_ref[0, :, :LANES], head)
    value = doubled(kv_ref[0, :, LANES:], head)
    key_t = kt_ref[pl.ds(pl.multiple_of(head * HEAD_SIZE, HEAD_SIZE), HEAD_SIZE), :]
    query, grad = q_ref[0], g_ref[0]
    mixed = (grad.astype(F32) * o_ref[0].astype(F32)).T
    dks, dvs, dqs = None, None, []
    for j in range(2):
        delta = jnp.sum(mixed[j * HEAD_SIZE : (j + 1) * HEAD_SIZE], axis=0, keepdims=True)
        dk, dv, dq = backward_columns(
            key,
            value,
            key_t,
            bias_ref,
            half_of(query, j),
            half_of(grad, j),
            lse_ref[0, 0, j : j + 1, :],
            delta,
            256,
        )
        dks = dk if dks is None else [a + b for a, b in zip(dks, dk)]
        dvs = dv if dvs is None else [a + b for a, b in zip(dvs, dv)]
        dqs.append(dq)
    dq_ref[0] = jnp.concatenate(dqs, axis=0).T * SCORE_SCALE
    add_into(dk_ref, folded(dks, head) * SCORE_SCALE, tile == 0)
    add_into(dv_ref, folded(dvs, head), tile == 0)


def prompt_backward(query, kv, out, grad, lse, start):
    groups, rows, query_width = query.shape
    length = kv.shape[1]
    tiles = query_width // LANES
    q_spec = pl.BlockSpec((1, rows, LANES), lambda g, t, s: (g, 0, t))
    k_spec = pl.BlockSpec((1, length, LANES), lambda g, t, s: (g, 0, 0))
    return pl.pallas_call(
        prompt_backward_kernel,
        out_shape=[
            jax.ShapeDtypeStruct(query.shape, F32),
            jax.ShapeDtypeStruct((groups, length, LANES), F32),
            jax.ShapeDtypeStruct((groups, length, LANES), F32),
        ],
        grid_spec=pltpu.PrefetchScalarGridSpec(
            num_scalar_prefetch=1,
            grid=(groups, tiles),
            in_specs=[
                q_spec,
                pl.BlockSpec((1, length, 2 * LANES), lambda g, t, s: (g, 0, 0)),
                q_spec,
                q_spec,
                pl.BlockSpec((1, 1, 2, rows), lambda g, t, s: (g, t, 0, 0)),
            ],
            out_specs=[q_spec, k_spec, k_spec],
            scratch_shapes=[pltpu.VMEM((LANES, length), BF), pltpu.VMEM((length, rows), F32)],
        ),
        compiler_params=params_of("arbitrary", "arbitrary"),
        cost_estimate=pl.CostEstimate(
            flops=20 * groups * tiles * rows * length * LANES,
            bytes_accessed=query.size * 10 + kv.size * 6,
            transcendentals=groups * tiles * 2 * rows * length,
        ),
        name="prompt_backward",
    )(start, query, kv, out, grad, lse)


def cont_backward_kernel(
    which,
    q_ref,
    kv_ref,
    own_ref,
    o_ref,
    g_ref,
    lse_ref,
    dq_ref,
    dk_ref,
    dv_ref,
    ek_ref,
    ev_ref,
    kt_ref,
    ot_ref,
):
    tile = pl.program_id(1)
    rows = q_ref.shape[1]
    head = tile // (pl.num_programs(1) // 2)

    @pl.when(tile == 0)
    def _():
        kt_ref[...] = kv_ref[0, :, :LANES].astype(F32).T.astype(BF)
        ot_ref[...] = own_ref[0, :, :LANES].astype(F32).T.astype(BF)

    place = pl.ds(pl.multiple_of(head * HEAD_SIZE, HEAD_SIZE), HEAD_SIZE)
    query, grad = q_ref[0], g_ref[0]
    mixed = (grad.astype(F32) * o_ref[0].astype(F32)).T
    delta = jnp.concatenate(
        [
            jnp.sum(mixed[j * HEAD_SIZE : (j + 1) * HEAD_SIZE], axis=0, keepdims=True)
            for j in range(2)
        ],
        axis=1,
    )
    queries = jnp.concatenate([half_of(query, 0), half_of(query, 1)], axis=0)
    grads = jnp.concatenate([half_of(grad, 0), half_of(grad, 1)], axis=0)
    bias = causal_bias(rows, rows, 0)
    lse = lse_ref[0, 0]
    dk, dv, dq = backward_columns(
        doubled(kv_ref[0, :, :LANES], head),
        doubled(kv_ref[0, :, LANES:], head),
        kt_ref[place, :],
        None,
        queries,
        grads,
        lse,
        delta,
        256,
    )
    ek, ev, eq = backward_columns(
        doubled(own_ref[0, :, :LANES], head),
        doubled(own_ref[0, :, LANES:], head),
        ot_ref[place, :],
        jnp.concatenate([bias, bias], axis=1),
        queries,
        grads,
        lse,
        delta,
        rows,
    )
    dq = dq + eq
    dq_ref[0] = jnp.concatenate([dq[:, :rows], dq[:, rows:]], axis=0).T * SCORE_SCALE
    add_into(dk_ref, folded(dk, head) * SCORE_SCALE, tile == 0)
    add_into(dv_ref, folded(dv, head), tile == 0)
    add_into(ek_ref, folded(ek, head) * SCORE_SCALE, tile == 0)
    add_into(ev_ref, folded(ev, head), tile == 0)


def cont_backward(query, kv, own, out, grad, lse, which):
    conts, rows, query_width = query.shape
    length = kv.shape[1]
    tiles = query_width // LANES
    q_spec = pl.BlockSpec((1, rows, LANES), lambda g, t, w: (g, 0, t))
    k_spec = pl.BlockSpec((1, length, LANES), lambda g, t, w: (g, 0, 0))
    e_spec = pl.BlockSpec((1, rows, LANES), lambda g, t, w: (g, 0, 0))
    return pl.pallas_call(
        cont_backward_kernel,
        out_shape=[jax.ShapeDtypeStruct(query.shape, F32)]
        + [jax.ShapeDtypeStruct((conts, length, LANES), F32)] * 2
        + [jax.ShapeDtypeStruct((conts, rows, LANES), F32)] * 2,
        grid_spec=pltpu.PrefetchScalarGridSpec(
            num_scalar_prefetch=1,
            grid=(conts, tiles),
            in_specs=[
                q_spec,
                pl.BlockSpec((1, length, 2 * LANES), lambda g, t, w: (w[g], 0, 0)),
                pl.BlockSpec((1, rows, 2 * LANES), lambda g, t, w: (g, 0, 0)),
                q_spec,
                q_spec,
                pl.BlockSpec((1, 1, 1, 2 * rows), lambda g, t, w: (g, t, 0, 0)),
            ],
            out_specs=[q_spec, k_spec, k_spec, e_spec, e_spec],
            scratch_shapes=[pltpu.VMEM((LANES, length), BF), pltpu.VMEM((LANES, rows), BF)],
        ),
        compiler_params=params_of("arbitrary", "arbitrary"),
        cost_estimate=pl.CostEstimate(
            flops=20 * conts * tiles * rows * (length + rows) * LANES,
            bytes_accessed=query.size * 10 + conts * length * LANES * 12,
            transcendentals=conts * tiles * 2 * rows * (length + rows),
        ),
        name="cont_backward",
    )(which, query, kv, own, out, grad, lse)


def finish_kernel(count, dq_ref, dkv_ref, *refs):
    others = refs[:count]
    q_ref, kv_ref, cosine, sine, out_ref, total_ref = refs[count:]
    query_width = dq_ref.shape[1]
    key_width = dkv_ref.shape[1] // 2
    dkv = dkv_ref[...]
    for other in others:
        dkv = dkv + other[...].astype(F32)
    dq = dq_ref[...]
    total_ref[...] = jnp.sum(dq * q_ref[...].astype(F32), axis=1, keepdims=True) + jnp.sum(
        dkv * kv_ref[...].astype(F32), axis=1, keepdims=True
    )
    back = -sine[...]
    for t in range(query_width // LANES):
        cut = slice(t * LANES, (t + 1) * LANES)
        out_ref[:, cut] = turn(dq[:, cut], cosine[...], back).astype(BF)
    out_ref[:, query_width : query_width + key_width] = turn(
        dkv[:, :key_width], cosine[...], back
    ).astype(BF)
    out_ref[:, query_width + key_width :] = dkv[:, key_width:].astype(BF)


def finish(dq, dkv, others, query, kv, tables):
    rows, query_width = dq.shape
    kv_width = dkv.shape[1]
    block = min(rows, 256)
    row = lambda w: pl.BlockSpec((block, w), lambda i: (i, 0))
    return pl.pallas_call(
        functools.partial(finish_kernel, len(others)),
        out_shape=[
            jax.ShapeDtypeStruct((rows, query_width + kv_width), BF),
            jax.ShapeDtypeStruct((rows, 1), F32),
        ],
        grid=(rows // block,),
        in_specs=[row(query_width)]
        + [row(kv_width)] * (1 + len(others))
        + [row(query_width), row(kv_width), row(LANES), row(LANES)],
        out_specs=[row(query_width + kv_width), row(1)],
        compiler_params=params_of("arbitrary"),
        cost_estimate=pl.CostEstimate(
            flops=20 * dq.size, bytes_accessed=dq.size * 12, transcendentals=0
        ),
        name="finish",
    )(dq, dkv, *others, query, kv, *tables)


def rope_tables(positions):
    lane = jnp.arange(LANES)
    half = HEAD_SIZE // 2
    frequency = ROPE_BASE ** (-(lane % half).astype(F32) * 2.0 / HEAD_SIZE)
    angles = positions.astype(F32)[:, None] * frequency[None, :]
    sign = jnp.where(lane % HEAD_SIZE < half, -1.0, 1.0)
    return jnp.cos(angles), jnp.sin(angles) * sign[None, :]


def second_norm_kernel(count, model_width, order, *refs):
    x, o = refs[:count], refs[count : 2 * count]
    gain, weight, out_ref, hidden_ref, scale_ref = refs[2 * count :]
    width, head_width = x[0].shape[1], o[0].shape[1]
    total = None
    for r, part in enumerate(o):
        term = dot_nn(part[...], weight[r * head_width : (r + 1) * head_width, :])
        total = term if total is None else total + term
    hidden_ref[...] = total
    places = [pl.ds(pl.multiple_of(order[r] * width, width), width) for r in range(count)]
    squares = 0.0
    for place, part in zip(places, x):
        h = hidden_ref[:, place] + part[...].astype(F32)
        hidden_ref[:, place] = h
        squares = squares + jnp.sum(h * h, axis=1, keepdims=True)
    scale = lax.rsqrt(squares / model_width + EPSILON)
    scale_ref[...] = scale
    for r, place in enumerate(places):
        out_ref[:, place] = (hidden_ref[:, place] * scale * gain[r : r + 1, :]).astype(BF)


def spread_kernel(count, order, *refs):
    parts = refs[:count]
    mix, out_ref = refs[count:]
    width = parts[0].shape[1]
    for r, part in enumerate(parts):
        place = pl.ds(pl.multiple_of(order[r] * width, width), width)
        out_ref[:, place] = (part[...].astype(F32) * mix[...]).astype(BF)


def third_norm_kernel(count, model_width, order, *refs):
    cot, n = refs[:count], refs[count : 2 * count]
    gain, scale_ref, mix, hidden_ref, out_ref, factor_ref = refs[2 * count :]
    width = cot[0].shape[1]
    places = [pl.ds(pl.multiple_of(order[r] * width, width), width) for r in range(count)]
    scale = scale_ref[...]
    total = 0.0
    for r, place in enumerate(places):
        total = total + jnp.sum(
            hidden_ref[:, place] * gain[r : r + 1, :] * n[r][...].astype(F32),
            axis=1,
            keepdims=True,
        )
    factor = scale * scale * scale * total / model_width
    factor_ref[...] = factor
    for r, place in enumerate(places):
        value = (
            cot[r][...].astype(F32) * mix[...]
            + scale * gain[r : r + 1, :] * n[r][...].astype(F32)
            - hidden_ref[:, place] * factor
        )
        out_ref[:, place] = value.astype(BF)


def placed_call(kernel, name, order, part_sets, wholes, columns_in, outs, flops=0):
    parts = [p for group in part_sets for p in group]
    rows, width = parts[0].shape
    block = min(rows, 256)
    row = lambda w: pl.BlockSpec((block, w), lambda i, o: (i, 0))
    return pl.pallas_call(
        kernel,
        out_shape=[jax.ShapeDtypeStruct((rows, w), d) for w, d in outs],
        grid_spec=pltpu.PrefetchScalarGridSpec(
            num_scalar_prefetch=1,
            grid=(rows // block,),
            in_specs=[row(p.shape[1]) for p in parts]
            + [pl.BlockSpec(w.shape, lambda i, o: (0, 0)) for w in wholes]
            + [row(c.shape[1]) for c in columns_in],
            out_specs=[row(w) for w, d in outs],
        ),
        compiler_params=params_of("arbitrary"),
        cost_estimate=pl.CostEstimate(
            flops=8 * len(parts) * rows * width + flops,
            bytes_accessed=2 * len(parts) * rows * width,
            transcendentals=rows,
        ),
        name=name,
    )(order, *parts, *wholes, *columns_in)


def second_norm(x, o, gains, weight, order):
    count, width = len(x), x[0].shape[1]
    return placed_call(
        functools.partial(second_norm_kernel, count, count * width),
        "second_norm",
        order,
        [x, o],
        [gains, weight],
        [],
        [(count * width, BF), (count * width, F32), (1, F32)],
        x[0].shape[0] * weight.size * 2,
    )


def spread(parts, mix, order):
    count, width = len(parts), parts[0].shape[1]
    return placed_call(
        functools.partial(spread_kernel, count),
        "spread",
        order,
        [parts],
        [],
        [mix],
        [(count * width, BF)],
    )[0]


def third_norm(hidden, cot, n, gains, scale, mix, order):
    count, width = len(cot), cot[0].shape[1]
    return placed_call(
        functools.partial(third_norm_kernel, count, count * width),
        "third_norm",
        order,
        [cot, n],
        [gains],
        [scale, mix, hidden],
        [(count * width, BF), (1, F32)],
    )


def body(
    prompt_in,
    cont_in,
    prompt_mask,
    cont_mask,
    cont_prompt,
    cont_start,
    gain_attn,
    gain_ffn,
    router,
    w_query,
    key_projection,
    w_value,
    w_out,
    w_gate,
    w_up,
    w_down,
    prompt_cot,
    cont_cot,
):
    groups, prompt_rows, width = prompt_in.shape
    conts = cont_in.shape[0]
    tp_size = lax.axis_size("tp")
    ctx_size = lax.axis_size("ctx")
    model_width = width * tp_size
    me_tp = lax.axis_index("tp")
    me_ctx = lax.axis_index("ctx")
    query_width = w_query.shape[1]
    key_width = key_projection.shape[1]
    kv_width = 2 * key_width
    streams = range(2)
    tokens_in = [prompt_in.reshape(-1, width), cont_in.reshape(-1, width)]
    cots = [prompt_cot.reshape(-1, width), cont_cot.reshape(-1, width)]
    masks = [prompt_mask.reshape(-1, 1).astype(F32), cont_mask.reshape(-1, 1).astype(F32)]
    prompt_place = me_ctx * prompt_rows + jnp.arange(prompt_rows, dtype=jnp.int32)
    cont_place = (
        cont_start[:, None] + jnp.arange(CONTINUATION_LEN, dtype=jnp.int32)[None, :]
    ).reshape(-1)
    tables = [rope_tables(jnp.tile(prompt_place, groups)), rope_tables(cont_place)]
    local_prompt = jnp.clip(cont_prompt - lax.axis_index("fsdp") * groups, 0, groups - 1)
    start = (me_ctx * prompt_rows).astype(jnp.int32)[None]
    order = jnp.stack([me_tp ^ step for step in range(tp_size)]).astype(jnp.int32)

    qkv_moves, lay_qkv = gather_weight(
        jnp.concatenate([w_query, key_projection, w_value], axis=1), 0
    )
    x_prompt, sent_prompt = gather_tp(tokens_in[0], qkv_moves[0])
    full_qkv = lay_qkv(None)
    small_params = tie(jnp.stack([gain_attn, gain_ffn, router]), x_prompt[2])
    params = [p.astype(F32) for p in pieces_of(small_params)]
    gains_attn = jnp.stack([p[0] for p in params])
    gains_ffn = jnp.stack([p[1] for p in params])
    routers = jnp.stack([p[2] for p in params])
    gate_moves, lay_gate = gather_weight(w_gate, 0, qkv_moves[0])
    up_moves, lay_up = gather_weight(w_up, 0, gate_moves[0])
    down_moves, lay_down = gather_weight(w_down, 1, up_moves[0])
    sent_out, out_moves, lay_out = gather_out(w_out, sent_prompt)
    x_cont, sent_cont = gather_tp(tie(tokens_in[1], sent_out))
    x_parts = [x_prompt, tie(x_cont, out_moves[1])]

    def enter(i):
        return entry(
            x_parts[i], gains_attn, routers, full_qkv, masks[i], tables[i], order, query_width
        )

    xn1, query, kv, scale_attn, gate_router, mixing = zip(enter(0), enter(1))
    own_kv = kv[0].reshape(groups, prompt_rows, kv_width)
    prompt_kv = jnp.zeros((groups, prompt_rows * ctx_size, kv_width), BF)
    for step, part in enumerate(pieces_of(own_kv, "ctx")):
        prompt_kv = lax.dynamic_update_slice(prompt_kv, part, (0, (me_ctx ^ step) * prompt_rows, 0))
    query = [tie(query[0], (sent_out, up_moves[0])), tie(query[1], (gate_moves[1], down_moves[0]))]
    full_out = lay_out(xn1[0])
    full_gate = lay_gate(xn1[0])
    full_up = lay_up(xn1[1])
    full_down = lay_down(xn1[1])
    queries = [
        query[0].reshape(groups, prompt_rows, query_width),
        query[1].reshape(conts, CONTINUATION_LEN, query_width),
    ]
    cont_kv = kv[1].reshape(conts, CONTINUATION_LEN, kv_width)
    prompt_o, prompt_lse = prompt_forward(queries[0], prompt_kv, start)
    cont_o, cont_lse = cont_forward(queries[1], prompt_kv, cont_kv, local_prompt)
    attended = [prompt_o.reshape(-1, query_width), cont_o.reshape(-1, query_width)]
    o_prompt, sent_prompt = gather_tp(attended[0])
    o_cont, sent_cont = gather_tp(
        tie(attended[1], (sent_prompt, out_moves, up_moves[1]))
    )

    def second(i, o):
        return second_norm(x_parts[i], o, gains_ffn, full_out, order)

    xn2_prompt, hidden_prompt, scale_prompt = second(0, o_prompt)
    cot_cont, sent_cont = gather_tp(tie(cots[1], sent_cont))
    xn2_cont, hidden_cont, scale_cont = second(1, o_cont)
    xn2, hidden, scale_ffn = (
        [xn2_prompt, xn2_cont],
        [hidden_prompt, hidden_cont],
        [scale_prompt, scale_cont],
    )

    def forward(i):
        g = product(xn2[i], full_gate)
        u = product(xn2[i], full_up)
        s = jax.nn.sigmoid(g)
        return g, u, s, (g * s * u).astype(BF)

    ahead = [forward(0), forward(1)]
    cot_prompt, sent_prompt = gather_tp(tie(cots[0], (sent_cont, xn2_prompt, down_moves[1])))
    cot_parts = [cot_prompt, cot_cont]

    inner, gate_grad, up_grad = [None, None], [None, None], [None, None]
    ffn_grad, blocks = [None, None], [None, None]
    for i in (1, 0):
        g, u, s, inner[i] = ahead[i]
        mix = mixing[i] if i == 1 else tie(mixing[i], blocks[1])
        ffn_grad[i] = spread(cot_parts[i], mix, order)
        dz = product_nt(ffn_grad[i], full_down)
        gate_grad[i] = (dz * u * s * (1.0 + g * (1.0 - s))).astype(BF)
        up_grad[i] = (dz * g * s).astype(BF)
        blocks[i] = blocks_of(
            lambda b, i=i: product_nt(gate_grad[i], rows_of(full_gate, b, width))
            + product_nt(up_grad[i], rows_of(full_up, b, width))
        )
        if i == 1:
            cont_sum, sent_cont = exchange_direct(blocks[1])

    both = lambda pair: jnp.concatenate(pair, axis=0)
    normed_grad = [None, cont_sum]
    blocks[0] = tie(blocks[0], cont_sum)
    normed_grad[0], sent_prompt = exchange_direct(blocks[0])
    n_cont = pieces_of(normed_grad[1].astype(BF))
    xn2_all, gate_all, up_all, inner_all, ffn_grad_all = tie(
        (both(xn2), both(gate_grad), both(up_grad), both(inner), both(ffn_grad)), blocks[0]
    )
    parts = [
        product_tn(xn2_all, gate_all).astype(BF),
        product_tn(xn2_all, up_all).astype(BF),
        product_tn(inner_all, ffn_grad_all).astype(BF),
    ]
    pieces = [scatter_grad(part, axis) for part, axis in zip(parts, (0, 0, 1))]
    late = tie(normed_grad[0].astype(BF), (n_cont, parts))
    n_prompt = pieces_of(late)
    n_parts = [n_prompt, n_cont]
    inner_late = tie(inner, parts)
    ffn_blocks = [
        blocks_of(lambda b, t=t: product(t, columns(full_down, b, width))) for t in inner_late
    ]

    def third(i):
        return third_norm(
            hidden[i], cot_parts[i], n_parts[i], gains_ffn, scale_ffn[i], mixing[i], order
        )

    dab_cont, factor_cont = third(1)
    do_cont = product_nt(dab_cont, full_out[:query_width]).astype(BF)
    dq_cont, dk_cont, dv_cont, dk_own, dv_own = cont_backward(
        queries[1],
        prompt_kv,
        cont_kv,
        cont_o,
        do_cont.reshape(queries[1].shape),
        cont_lse,
        local_prompt,
    )
    dab_prompt, factor_prompt = third(0)
    do_prompt = product_nt(dab_prompt, full_out[:query_width]).astype(BF)
    dab, factor = [dab_prompt, dab_cont], [factor_prompt, factor_cont]
    ffn_blocks = tie(ffn_blocks, n_prompt)
    branch_ffn = [None, None]
    branch_ffn[1], sent_cont = exchange_direct(ffn_blocks[1])
    branch_ffn[0], sent_prompt = exchange_direct(ffn_blocks[0])
    across = [swap(p, "ctx", 2) if paired() else p for p in pieces]
    dq_prompt, dk_prompt, dv_prompt = prompt_backward(
        queries[0], prompt_kv, prompt_o, do_prompt.reshape(queries[0].shape), prompt_lse, start
    )
    dq_prompt = tie(dq_prompt, branch_ffn[1])
    started_out = grad_start(both(attended), tie(both(dab), dq_prompt), 1)
    chosen = (local_prompt[:, None] == jnp.arange(groups, dtype=jnp.int32)[None, :]).astype(F32)

    def kv_block(step):
        place = (me_ctx ^ step) * prompt_rows

        def piece(whole):
            return lax.dynamic_slice(
                whole, (0, place, 0), (whole.shape[0], prompt_rows, whole.shape[2])
            )

        def total(prompts, extra):
            extra = piece(extra)
            sums = [
                sum(chosen[c, g] * extra[c] for c in range(conts)) for g in range(groups)
            ]
            return piece(prompts) + jnp.stack(sums)

        return jnp.concatenate(
            [total(dk_prompt, dk_cont), total(dv_prompt, dv_cont)], axis=2
        ).reshape(-1, kv_width)

    sent = [swap(kv_block(step).astype(BF), "ctx", step) for step in range(1, ctx_size)]
    dkv_own = jnp.concatenate([dk_own, dv_own], axis=2).reshape(-1, kv_width)
    finished_cont = finish(
        dq_cont.reshape(-1, query_width), dkv_own, [], query[1], kv[1], tables[1]
    )
    finished = [
        finish(dq_prompt.reshape(-1, query_width), kv_block(0), sent, query[0], kv[0], tables[0]),
        finished_cont,
    ]
    dqkv = [f[0] for f in finished]
    attn_blocks = [
        blocks_of(lambda b, t=t: product_nt(t, rows_of(full_qkv, b, width))) for t in dqkv
    ]
    qkv_left, qkv_right = tie((both(xn1), both(dqkv)), attn_blocks)
    started_qkv = grad_start(qkv_left, qkv_right, 0)
    normed_attn_grad = [None, None]
    normed_attn_grad[1], relay_cont, _ = exchange_sum(
        tie(attn_blocks[1], sent_prompt), across[0]
    )
    sizes = [t.shape[0] for t in dqkv]
    joined = lambda pair: jnp.concatenate([p.reshape(-1, LANES) for p in pair], axis=0)
    parted = lambda t: [
        p.reshape(-1, 1) for p in jnp.split(t, [sizes[0] // LANES], axis=0)
    ]
    total_attn = parted(all_sum(joined([f[1] for f in finished])))
    grad_out = grad_end(grad_middle(*started_out, 1), 1)
    grad_qkv = grad_end(grad_middle(*started_qkv, 0), 0)
    grad_gate, grad_up, grad_down = [
        spread_grad(piece, far, axis) for piece, far, axis in zip(pieces, across, (0, 0, 1))
    ]

    gain_attn_sum, gain_ffn_sum, router_sum = 0.0, 0.0, 0.0
    outs, token_grads = [], []
    hidden_own = [columns(h, me_tp, width) for h in hidden]
    branch = [
        hidden_own[i] - tokens_in[i].astype(F32) + branch_ffn[i] for i in streams
    ]
    sums = parted(
        all_sum(
            joined(
                [
                    jnp.sum(cots[i].astype(F32) * mixing[i] * branch[i], axis=1, keepdims=True)
                    for i in streams
                ]
            )
        )
    )
    normed_attn_grad[0] = exchange_sum(
        tie(attn_blocks[0], (relay_cont, branch_ffn[0])),
        (sums, total_attn, across[1]),
    )[0]
    for i in streams:
        x = tokens_in[i].astype(F32)
        dy = cots[i].astype(F32)
        outs.append((x + mixing[i] * branch[i]).astype(BF))
        dl = (1.0 - gate_router[i]) * sums[i]
        router_sum = router_sum + jnp.sum(x * dl, axis=0)
        gain_ffn_sum = gain_ffn_sum + jnp.sum(
            hidden_own[i] * scale_ffn[i] * normed_grad[i], axis=0
        )
        back_ffn = scale_ffn[i] * gains_ffn[0:1] * normed_grad[i] - hidden_own[i] * factor[i]
        scale = scale_attn[i]
        n = normed_attn_grad[i]
        gain_attn_sum = gain_attn_sum + jnp.sum(x * scale * n, axis=0)
        n1 = scale * gains_attn[0:1] * n - x * (scale * scale * total_attn[i] / model_width)
        token_grads.append(dy + dl * routers[0:1] + back_ffn + n1)
    small = group_sum(jnp.stack([gain_attn_sum, gain_ffn_sum, router_sum]))
    return (
        outs[0].reshape(prompt_in.shape),
        outs[1].reshape(cont_in.shape),
        token_grads[0].reshape(prompt_in.shape),
        token_grads[1].reshape(cont_in.shape),
        small[0],
        small[1],
        small[2],
        grad_qkv[:, :query_width],
        grad_qkv[:, query_width : query_width + key_width],
        grad_qkv[:, query_width + key_width :],
        grad_out,
        grad_gate,
        grad_up,
        grad_down,
    )


def solution(mesh):
    placed = (
        P("fsdp", "ctx", "tp"),
        P(("fsdp", "ctx"), None, "tp"),
        P("fsdp", "ctx"),
        P(("fsdp", "ctx"), None),
        P(("fsdp", "ctx")),
        P(("fsdp", "ctx")),
        P("tp"),
        P("tp"),
        P("tp"),
        P("fsdp", "tp"),
        P("fsdp", "tp"),
        P("fsdp", "tp"),
        P("tp", "fsdp"),
        P("fsdp", "tp"),
        P("fsdp", "tp"),
        P("tp", "fsdp"),
        P("fsdp", "ctx", "tp"),
        P(("fsdp", "ctx"), None, "tp"),
    )
    return jax.shard_map(
        body,
        mesh=mesh,
        in_specs=placed,
        out_specs=(
            P("fsdp", "ctx", "tp"),
            P(("fsdp", "ctx"), None, "tp"),
            P("fsdp", "ctx", "tp"),
            P(("fsdp", "ctx"), None, "tp"),
            P("tp"),
            P("tp"),
            P("tp"),
            P("fsdp", "tp"),
            P("fsdp", "tp"),
            P("fsdp", "tp"),
            P("tp", "fsdp"),
            P("fsdp", "tp"),
            P("fsdp", "tp"),
            P("tp", "fsdp"),
        ),
        check_vma=False,
    )
```
